32 devices in a mesh: field: 2 (over x), cap: 4 (over y, core), bank: 4 (over z).
Axes of the slice: x: 2, y: 2, z: 4, core: 2. Of those that a mesh axis runs over, the one named last changes fastest.
Arguments:
- pattern: bfloat16 [4, 3, 542, 512], P('cap', None, None, 'field'), may hold values from -6 to 6
- measured: bfloat16 [4, 3, 32, 512], P('cap', None, None, 'field'), may hold values from -6 to 6
- row_kernels: bfloat16 [4, 3, 16, 511], P('field', None, 'bank'), may hold values from -0.125 to 0.125
- col_kernels: bfloat16 [4, 3, 16, 511], P('field', None, 'bank'), may hold values from -0.125 to 0.125
- tile_patch: int32 [4], P('field'), may hold values from 0 to 1
- sat_tiles: int32 [4, 256], P('cap'), may hold values from 0 to 63
Outputs:
- grad_rows: float32 [4, 3, 16, 511], P('field', None, 'bank')
- grad_cols: float32 [4, 3, 16, 511], P('field', None, 'bank')
The draws below stay inside these ranges and needn't reach their ends.
Inputs may be any that keep to these rules, and one draw needn't show every extreme that they name: Patch t of the window uses kernel set (t // 2) * 2 + tile_patch[t]. `sat_tiles`: tile numbers run row by row over tiles of 16 x 16 pixels of the window; an entry may repeat.
All inputs are finite; a program needn't handle non-finite values.
Results may differ from the reference program's by a relative error of at most 0.0033.
Values may be sent and summed in bfloat16 or wider, within the bound.
No kernel may reach another device: no remote copies, remote signals or barrier semaphores. Data moves between devices by JAX's collectives and lax.ppermute only.
A program may use at most 64 MiB of HBM per device.

```python
import math
import jax
import jax.numpy as jnp
import numpy as np
from jax import lax

TAPS = 511
RANKS = 16
COLOURS = 3
PW = 128
PATCH_DEV = 2
H = 32
TILE = 16
NSAT = 256
HALF = 255
R = 542
NX = 512
NPATCH = 4
CAPS = 4
NTILES = 64


def plant(drawn, rng, least, high):
    longest = drawn.shape.index(max(drawn.shape))
    spots = []
    for shift in (0, 1):
        where = [jax.random.randint(jax.random.fold_in(rng, axis), (), 0, length) for axis, length in enumerate(drawn.shape)]
        where[longest] = (where[longest] + shift) % drawn.shape[longest]
        spots.append(tuple(where))
    return drawn.at[spots[0]].set(least).at[spots[1]].set(high)


def levels(key, dims, cuts, least, top_value):
    def one(axis_at, blocks):
        draws = jax.random.uniform(jax.random.fold_in(jax.random.fold_in(key, 6), axis_at), (blocks,), jnp.float32, least / len(cuts), top_value / len(cuts))
        return jnp.repeat(jnp.exp(draws), dims[axis_at] // blocks).reshape((-1,) + (1,) * (len(dims) - axis_at - 1))

    loudness = one(*cuts[0])
    for cut in cuts[1:]:
        loudness = loudness * one(*cut)
    return loudness


def rank_bounds(amount, skew):
    portions = [(1 << 20) // math.isqrt(standing ** skew) + 1 for standing in range(1, amount + 1)]
    width = 1 + sum(portions) // (1 << 30)
    return np.cumsum(np.array([max(1, weight // width) for weight in portions]))


def skewed_ids(own_key, shape, count, lean):
    listing = rank_bounds(count, lean)
    ticket = jax.random.randint(jax.random.fold_in(own_key, 1), shape, 0, int(listing[count - 1]))
    rank = jnp.searchsorted(jnp.asarray(listing, jnp.int32), ticket, side="right")
    return jax.random.permutation(jax.random.fold_in(own_key, 2), count)[rank].astype(jnp.int32)


def bell_draw(key, extent, scale, limit, pieces=(), kind=jnp.bfloat16):
    drawn = scale * jax.random.normal(key, extent, jnp.float32)
    if pieces:
        drawn = drawn * levels(key, extent, pieces, -0.22, 0.18)
    return jnp.clip(drawn, -limit, limit).astype(kind)


def setup_inputs(seed: int = 0) -> dict:
    streams_of = jax.random.split(jax.random.key(seed), 7)
    return {
        "pattern": bell_draw(streams_of[0], (CAPS, COLOURS, R, NX), 1.0, 6.0, ((0, 4), (3, 2))),
        "measured": bell_draw(streams_of[1], (CAPS, COLOURS, H, NX), 1.0, 6.0, ((0, 4), (3, 2))),
        "row_kernels": bell_draw(streams_of[2], (NPATCH, COLOURS, RANKS, TAPS), (4 * TAPS) ** -0.5, 0.125, ((0, 2), (2, 4))),
        "col_kernels": bell_draw(streams_of[3], (NPATCH, COLOURS, RANKS, TAPS), (4 * TAPS) ** -0.5, 0.125, ((0, 2), (2, 4))),
        "tile_patch": plant(jax.random.randint(streams_of[4], (NPATCH,), 0, PATCH_DEV), jax.random.fold_in(streams_of[4], 1), 0, PATCH_DEV - 1).astype(jnp.int32),
        "sat_tiles": plant(skewed_ids(streams_of[5], (CAPS, NSAT), NTILES, 2), jax.random.fold_in(streams_of[5], 3), 0, NTILES - 1).astype(jnp.int32),
    }


def banded(kernel, band_width):
    tap_count = kernel.shape[-1]
    span_len = band_width + tap_count - 1
    zero_tail = jnp.zeros(kernel.shape[:-1] + (band_width,), kernel.dtype)
    padded = jnp.concatenate([kernel, zero_tail], axis=-1)
    repeated = jnp.tile(padded, (1,) * (kernel.ndim - 1) + (band_width,))
    return repeated[..., : band_width * span_len].reshape(kernel.shape[:-1] + (band_width, span_len))


def diagonals(matrix, tap_count):
    line_count = matrix.shape[-2]
    span_len = matrix.shape[-1]
    flattened = matrix.reshape(matrix.shape[:-2] + (line_count * span_len,))
    zero_tail = jnp.zeros(matrix.shape[:-2] + (line_count,), matrix.dtype)
    flattened = jnp.concatenate([flattened, zero_tail], axis=-1)
    shaped = flattened.reshape(matrix.shape[:-2] + (line_count, span_len + 1))
    return jnp.sum(shaped[..., :tap_count], axis=-2)


def reference(pattern, measured, row_kernels, col_kernels, tile_patch, sat_tiles):
    extended = jnp.pad(pattern, ((0, 0), (0, 0), (0, 0), (HALF, HALF)))
    tile_ids = (jnp.arange(H // TILE, dtype=jnp.int32)[:, None] * (NX // TILE)
                + jnp.arange(NX // TILE, dtype=jnp.int32)[None, :]).astype(jnp.int32)
    saturated = jnp.any(tile_ids[None, :, :, None] == sat_tiles[:, None, None, :], axis=-1)
    keep_tiles = 1.0 - saturated.astype(jnp.float32)
    keep_pixels = jnp.broadcast_to(keep_tiles[:, :, None, :, None],
                                   (CAPS, H // TILE, TILE, NX // TILE, TILE)).reshape(CAPS, H, NX)
    patch_ids = jnp.arange(NPATCH, dtype=jnp.int32)
    kernel_sets = ((patch_ids // PATCH_DEV) * PATCH_DEV + tile_patch).astype(jnp.int32)

    def one_tile(tile_index):
        chosen = kernel_sets[tile_index]
        row_taps = row_kernels[chosen]
        col_taps = col_kernels[chosen]
        start = (tile_index * PW).astype(jnp.int32)
        window_cols = lax.dynamic_slice_in_dim(extended, start, PW + 2 * HALF, 3).astype(jnp.float32)
        row_band = banded(row_taps, PW).astype(jnp.float32)
        col_band = banded(col_taps, H).astype(jnp.float32)
        rowpass = jnp.einsum("cqyj,qrxj->cqryx", window_cols, row_band).astype(jnp.bfloat16)
        rowpass_wide = rowpass.astype(jnp.float32)
        predicted = jnp.einsum("qryk,cqrkx->cqyx", col_band, rowpass_wide)
        measured_tile = lax.dynamic_slice_in_dim(measured, start, PW, 3).astype(jnp.float32)
        keep_tile = lax.dynamic_slice_in_dim(keep_pixels, start, PW, 2)
        residual = (keep_tile[:, None] * (predicted - measured_tile)).astype(jnp.bfloat16)
        residual_wide = residual.astype(jnp.float32)
        backward = jnp.einsum("qryk,cqyx->cqrkx", col_band, residual_wide).astype(jnp.bfloat16)
        row_terms = jnp.einsum("cqrkx,cqkj->qrxj", backward.astype(jnp.float32), window_cols)
        col_terms = jnp.einsum("cqyx,cqrkx->qryk", residual_wide, rowpass_wide)
        return diagonals(row_terms, TAPS), diagonals(col_terms, TAPS)

    per_row, per_col = lax.map(one_tile, patch_ids)
    grad_rows = jax.ops.segment_sum(per_row, kernel_sets, num_segments=NPATCH) * (1.0 / H)
    grad_cols = jax.ops.segment_sum(per_col, kernel_sets, num_segments=NPATCH) * (1.0 / H)
    return grad_rows, grad_cols
```

```python
import functools

import jax
import jax.numpy as jnp
from jax import lax
from jax.experimental import pallas as pl
from jax.experimental.pallas import tpu as pltpu
from jax.sharding import PartitionSpec as P

TILE = 16
BF = jnp.bfloat16
F32 = jnp.float32
NT = (((1,), (1,)), ((), ()))
NN = (((1,), (0,)), ((), ()))
TN = (((0,), (0,)), ((), ()))


def dot(a, b, dims):
    return lax.dot_general(a, b, dims, preferred_element_type=F32)


def exchange(cells, axis, step):
    count = lax.axis_size(axis)
    return lax.ppermute(cells, axis, [(i, i ^ step) for i in range(count)])


def pad_rows(dst, lanes, rows_ref, rows):
    width = rows_ref.shape[-1]
    depth = dst.shape[0]
    whole = rows // 16 * 16
    dst[whole:depth, lanes : lanes + width] = jnp.zeros((depth - whole, width), BF)
    dst[0:rows, lanes : lanes + width] = rows_ref[...]


def triangle(side, patch, width, strip):
    x = lax.broadcasted_iota(jnp.int32, (width, strip), 0) + patch * width
    j = lax.broadcasted_iota(jnp.int32, (width, strip), 1)
    left = (j > x).astype(jnp.int32)
    right = (j < x).astype(jnp.int32)
    return (side * left + (1 - side) * right) > 0


def front(
    dims, scalars, w_ref, *refs
):
    pieces, n_nb, tiles, width, strip, rows, height = dims
    kern = refs[: len(pieces)]
    band_nb, band_own, cols_out, v_own, pred, wp, band_all, vl = refs[len(pieces) :]
    lanes = 2 * strip
    depth = wp.shape[0]
    pad_rows(wp, 0, w_ref.at[0, 0], rows)
    for t in range(tiles):
        pick = scalars[t]
        masks = [triangle(scalars[tiles + n], t, width, strip) for n in range(n_nb)]
        slot = 0
        for piece, slots in zip(kern, pieces):
            for s in range(slots):
                row_taps = piece[s, 0, pick, 0].astype(F32)
                col_taps = piece[s, 1, pick, 0].astype(F32)
                ranks = row_taps.shape[0]
                col_taps = jnp.concatenate(
                    [col_taps, jnp.zeros((ranks, depth - col_taps.shape[1]), F32)], axis=1
                )
                for r in range(ranks):
                    at = slot * strip
                    one = jnp.broadcast_to(row_taps[r : r + 1], (16, lanes))
                    base = pltpu.roll(one, 1 + t * width, 1, stride=1, stride_axis=0).astype(BF)
                    for g in range(width // 16):
                        tile = base if g == 0 else pltpu.roll(base, 16 * g, 1)
                        span = slice(16 * g, 16 * g + 16)
                        for n in range(n_nb):
                            kept = jnp.where(masks[n][span], tile[:, :strip].astype(F32), 0.0)
                            band_nb[0, n, t, span, at : at + strip] = kept.astype(BF)
                        band_all[span, at : at + strip] = tile[:, strip:]
                    one = jnp.broadcast_to(col_taps[r : r + 1], (height, depth))
                    cols = pltpu.roll(one, 0, 1, stride=1, stride_axis=0).astype(BF)
                    cols_out[0, t, slot * height : (slot + 1) * height, :] = cols
                    slot += 1
        keep = band_own.shape[-1]
        band_own[0, t] = band_all[:, :keep]
        v = dot(cols_out[0, t], wp[...], NN).astype(BF)
        for r in range(slot):
            vl[:, r * strip : (r + 1) * strip] = v[r * height : (r + 1) * height]
        v_own[0, t] = vl[:, :keep]
        pred[0, t * width : (t + 1) * width, :] = dot(band_all[...], vl[...], NT)


def fold(rows, shift_groups):
    total = rows[0:8]
    for g in range(1, rows.shape[0] // 8):
        total = total + pltpu.roll(rows[8 * g : 8 * g + 8], rows.shape[1] - 8 * g, 1)
    return total


def settle(acc):
    count, lanes = acc.shape
    sub = lax.broadcasted_iota(jnp.int32, acc.shape, 0)
    for bit in (1, 2, 4):
        acc = jnp.where((sub & bit) != 0, pltpu.roll(acc, lanes - bit, 1), acc)
    return jnp.sum(acc.reshape(count // 8, 8, lanes), axis=1)


def back(dims, scalars, w_own, *refs):
    n_nb, tiles, width, strip, rows, height, ranks, scale = dims
    halos = refs[:n_nb]
    (band_nb, band_own, cols, v_own, pred, base, keep, out, wp, vl, vn, us, acc) = refs[n_nb:]
    all_ranks = cols.shape[2] // height
    lanes = 2 * strip
    for n in range(n_nb):
        pad_rows(wp, n * strip, halos[n].at[0, 0], rows)
    pad_rows(wp, n_nb * strip, w_own.at[0, 0], rows)
    for t in range(tiles):
        span = slice(t * width, (t + 1) * width)
        total = pred[0, span, :]
        for n in range(n_nb):
            v = dot(cols[0, t], wp[:, n * strip : (n + 1) * strip], NN).astype(BF)
            for r in range(all_ranks):
                vl[:, r * strip : (r + 1) * strip] = v[r * height : (r + 1) * height]
            vn[n] = vl[:, : ranks * strip]
            total = total + dot(band_nb[0, n, t], vl[...], NT)
        res_t = (keep[span, :] * (total - base[0, span, :])).astype(BF)
        for r in range(ranks):
            at = slice(r * strip, (r + 1) * strip)
            near = dot(res_t, v_own[0, t, :, at], NN)
            far = jnp.zeros((width, strip), F32)
            for n in range(n_nb):
                mask = triangle(scalars[tiles + n], t, width, strip)
                far = far + jnp.where(mask, dot(res_t, vn[n, :, at], NN), 0.0)
            both = jnp.concatenate([far, near], axis=1)
            part = fold(both, 0)
            acc[8 * (t * ranks + r) : 8 * (t * ranks + r) + 8, :lanes] = pltpu.roll(
                part, lanes - (t * width + 1), 1
            )
        for n in range(n_nb + 1):
            bands = band_own[0, t] if n == n_nb else band_nb[0, n, t, :, : ranks * strip]
            u = dot(res_t, bands, TN).astype(BF)
            for r in range(ranks):
                first = (t * ranks + r) * height
                us[first : first + height, n * strip : (n + 1) * strip] = u[
                    :, r * strip : (r + 1) * strip
                ]
    row_grads = settle(acc[...]) * scale
    z = dot(us[...], wp[...], NT)
    for i in range(tiles * ranks):
        acc_z = fold(z[i * height : (i + 1) * height], 0)
        wp_z = settle(acc_z)
        col = wp_z[:, :lanes] * scale
        row = row_grads[i : i + 1]
        t, r = divmod(i, ranks)
        for s in range(tiles):
            hit = (scalars[t] == s).astype(F32)
            if t == 0:
                out[0, 0, s, r : r + 1, :] = hit * row
                out[0, 1, s, r : r + 1, :] = hit * col
            else:
                out[0, 0, s, r : r + 1, :] += hit * row
                out[0, 1, s, r : r + 1, :] += hit * col


def body(pattern, measured, row_kernels, col_kernels, tile_patch, sat_tiles):
    _, colours, rows, strip = pattern.shape
    height = measured.shape[2]
    tiles, _, ranks, taps = row_kernels.shape
    width = strip // tiles
    lanes = 2 * strip
    depth = -(-rows // 128) * 128
    fields = lax.axis_size("field")
    banks = lax.axis_size("bank")
    caps = lax.axis_size("cap")
    here = lax.axis_index("field")

    if fields == 2:
        halos = [exchange(pattern, "field", 1)]
        sides = [here]
    else:
        halos = [
            lax.ppermute(pattern, "field", [(i, i + 1) for i in range(fields - 1)]),
            lax.ppermute(pattern, "field", [(i + 1, i) for i in range(fields - 1)]),
        ]
        sides = [jnp.ones_like(here), jnp.zeros_like(here)]
    n_nb = len(halos)

    kern = jnp.stack([row_kernels, col_kernels])
    kern = jnp.pad(kern, ((0, 0),) * 4 + ((0, lanes - taps),))[None]
    pieces = [kern]
    step = 1
    while step < banks:
        held = pieces[0] if len(pieces) == 1 else jnp.concatenate(pieces, axis=0)
        pieces.append(exchange(held, "bank", step))
        step *= 2
    counts = tuple(p.shape[0] for p in pieces)
    all_ranks = sum(counts) * ranks

    scalars = jnp.concatenate([tile_patch, jnp.stack(sides).astype(jnp.int32)])

    strip_tiles = strip // TILE
    across = strip_tiles * fields
    row_ids = jnp.arange(height // TILE, dtype=jnp.int32)
    col_ids = here * strip_tiles + jnp.arange(strip_tiles, dtype=jnp.int32)
    tile_ids = col_ids[:, None] + row_ids[None, :] * across
    saturated = jnp.any(tile_ids[:, :, None] == sat_tiles[0][None, None, :], axis=-1)
    keep = 1.0 - saturated.astype(F32)
    keep = jnp.broadcast_to(
        keep[:, None, :, None], (strip_tiles, TILE, height // TILE, TILE)
    ).reshape(strip, height)
    base = jnp.swapaxes(measured[0], 1, 2).astype(F32)

    vmem = pltpu.VMEM
    params = pltpu.CompilerParams(
        dimension_semantics=("arbitrary",), vmem_limit_bytes=40 * 2**20
    )

    def per_colour(shape):
        nd = len(shape)
        return pl.BlockSpec((1,) + shape, lambda q, *_: (q,) + (0,) * nd)

    smem = pl.BlockSpec(memory_space=pltpu.SMEM)
    w_spec = pl.BlockSpec((1, 1, rows, strip), lambda q: (0, q, 0, 0))
    band_nb_s = (n_nb, tiles, width, all_ranks * strip)
    band_own_s = (tiles, width, ranks * strip)
    cols_s = (tiles, all_ranks * height, depth)
    v_own_s = (tiles, height, ranks * strip)
    pred_s = (strip, height)
    shapes = [
        (band_nb_s, BF),
        (band_own_s, BF),
        (cols_s, BF),
        (v_own_s, BF),
        (pred_s, F32),
    ]
    fronts = pl.pallas_call(
        functools.partial(front, (counts, n_nb, tiles, width, strip, rows, height)),
        grid=(colours,),
        in_specs=[smem, w_spec]
        + [
            pl.BlockSpec((c, 2, tiles, 1, ranks, lanes), lambda q: (0, 0, 0, q, 0, 0))
            for c in counts
        ],
        out_specs=[per_colour(s) for s, _ in shapes],
        out_shape=[jax.ShapeDtypeStruct((colours,) + s, d) for s, d in shapes],
        scratch_shapes=[
            vmem((depth, strip), BF),
            vmem((width, all_ranks * strip), BF),
            vmem((height, all_ranks * strip), BF),
        ],
        compiler_params=params,
        name="front",
    )(scalars, pattern, *pieces)

    out_s = (2, tiles, ranks, lanes)
    grads = pl.pallas_call(
        functools.partial(
            back, (n_nb, tiles, width, strip, rows, height, ranks, 1.0 / height)
        ),
        grid=(colours,),
        in_specs=[smem, w_spec]
        + [w_spec] * n_nb
        + [per_colour(s) for s, _ in shapes]
        + [per_colour(pred_s), pl.BlockSpec((strip, height), lambda q: (0, 0))],
        out_specs=per_colour(out_s),
        out_shape=jax.ShapeDtypeStruct((colours,) + out_s, F32),
        scratch_shapes=[
            vmem((depth, (n_nb + 1) * strip), BF),
            vmem((height, all_ranks * strip), BF),
            vmem((n_nb, height, ranks * strip), BF),
            vmem((tiles * ranks * height, (n_nb + 1) * strip), BF),
            vmem((8 * tiles * ranks, lanes), F32),
        ],
        compiler_params=params,
        name="back",
    )(scalars, pattern, *halos, *fronts, base, keep)

    step = caps // 2
    while step:
        grads = grads + exchange(grads, "cap", step)
        step //= 2
    grads = jnp.moveaxis(grads, 0, 2)[..., :taps]
    return grads[0], grads[1]


def solution(mesh):
    return jax.shard_map(
        body,
        mesh=mesh,
        in_specs=(
            P("cap", None, None, "field"),
            P("cap", None, None, "field"),
            P("field", None, "bank", None),
            P("field", None, "bank", None),
            P("field"),
            P("cap", None),
        ),
        out_specs=(P("field", None, "bank", None), P("field", None, "bank", None)),
        check_vma=False,
    )
```

```python
import functools

import jax
import jax.numpy as jnp
from jax import lax
from jax.experimental import pallas as pl
from jax.experimental.pallas import tpu as pltpu
from jax.sharding import PartitionSpec as P

TILE = 16
BF = jnp.bfloat16
F32 = jnp.float32


def mm(a, b):
    return jnp.dot(a, b, preferred_element_type=F32)


def split(v):
    high = v.astype(BF)
    return high, (v - high.astype(F32)).astype(BF)


def exchange(cells, axis, step):
    count = lax.axis_size(axis)
    return lax.ppermute(cells, axis, [(i, i ^ step) for i in range(count)])


def fill(dst, at, cells):
    rows, width = cells.shape
    depth = dst.shape[0]
    whole = rows // 16 * 16
    dst[whole:depth, at : at + width] = jnp.zeros((depth - whole, width), BF)
    dst[0:rows, at : at + width] = cells


def below(side, j, x):
    left = (j > x).astype(jnp.int32)
    right = (j < x).astype(jnp.int32)
    return (side * left + (1 - side) * right) > 0


def front(dims, scalars, w_ref, *refs):
    count, own, colours, n_nb, tiles, width, strip, rows, height, ranks = dims
    kern = refs[:count]
    band_nb, cols, pred = refs[count : count + 3]
    if own:
        cat_own, cat_nb, v_own = refs[count + 3 : count + 6]
    wp, band, vl, masks = refs[-4:]
    lanes = 2 * strip
    depth = wp.shape[0]
    groups = width // 16
    wide = lanes // width
    for n in range(n_nb):
        for t in range(tiles):
            j = lax.broadcasted_iota(jnp.int32, (strip, width), 0)
            x = lax.broadcasted_iota(jnp.int32, (strip, width), 1) + t * width
            masks[n, t] = below(scalars[tiles + n], j, x).astype(F32).astype(BF)

    @pl.loop(0, colours)
    def _(q):
        fill(wp, 0, w_ref[0, q])
        for t in range(tiles):
            pick = scalars[t]
            for p in range(count):
                row_taps = kern[p][0, pick, q].astype(F32)
                col_taps = kern[p][1, pick, q].astype(F32)
                col_taps = jnp.concatenate(
                    [col_taps, jnp.zeros((ranks, depth - lanes), F32)], axis=1
                )
                for r in range(ranks):
                    slot = p * ranks + r
                    one = jnp.broadcast_to(row_taps[r : r + 1], (16, lanes))
                    base = pltpu.roll(one, 0, 1, stride=1, stride_axis=0).astype(BF)
                    for b in range(groups):
                        turned = base if b == 0 else pltpu.roll(base, 16 * b, 1)
                        for a in range(wide):
                            at = (t - a) % wide * width
                            tile = turned[:, at : at + width]
                            j = 16 * (groups * a + b)
                            if j < strip:
                                for n in range(n_nb):
                                    kept = tile * masks[n, t, j : j + 16, :]
                                    first = slot * strip + j
                                    band_nb[q, n, t, first : first + 16, :] = kept
                                    if own:
                                        side = (t * ranks + r) * width
                                        cat_nb[q, n, j : j + 16, side : side + width] = kept
                            else:
                                j -= strip
                                first = slot * strip + j
                                band[first : first + 16, :] = tile
                                if own:
                                    side = (t * ranks + r) * width
                                    cat_own[q, j : j + 16, side : side + width] = tile
                    one = jnp.broadcast_to(col_taps[r : r + 1], (16, depth))
                    base = pltpu.roll(one, 0, 1, stride=1, stride_axis=0).astype(BF)
                    for b in range(height // 16):
                        first = slot * height + 16 * b
                        turned = base if b == 0 else pltpu.roll(base, 16 * b, 1)
                        cols[q, t, first : first + 16, :] = turned
            v = mm(cols[q, t], wp[...])
            high, low = split(v)
            for r in range(count * ranks):
                span = slice(r * height, (r + 1) * height)
                vl[:, r * strip : (r + 1) * strip] = high[span]
                if own:
                    v_own[q, t, r, 0:height, :] = high[span]
                    v_own[q, t, r, height : 2 * height, :] = low[span]
            pred[q, t] = mm(vl[...], band[...])


def fold(rows):
    lanes = rows.shape[1]
    total = rows[0:8]
    for g in range(1, rows.shape[0] // 8):
        total = total + pltpu.roll(rows[8 * g : 8 * g + 8], lanes - 8 * g, 1)
    return total


def settle(acc):
    count, lanes = acc.shape
    sub = lax.broadcasted_iota(jnp.int32, acc.shape, 0)
    for bit in (1, 2, 4):
        acc = jnp.where((sub & bit) != 0, pltpu.roll(acc, lanes - bit, 1), acc)
    return jnp.sum(acc.reshape(count // 8, 8, lanes), axis=1)


def back(dims, scalars, w_own, meas, keep, *refs):
    q, n_nb, groups, tiles, width, strip, rows, height, ranks, scale = dims
    halos = refs[:n_nb]
    at = n_nb
    parts = []
    for _ in range(groups):
        parts.append(refs[at : at + 3])
        at += 3
    cat_own, cat_nb, v_own = refs[at : at + 3]
    out, wp, vl, vn, spread, us, acc, acc_z = refs[at + 3 :]
    lanes = 2 * strip
    for n in range(n_nb):
        fill(wp, n * strip, halos[n][0, 0])
    fill(wp, n_nb * strip, w_own[0, q])
    block = lax.broadcasted_iota(jnp.int32, (width, width), 1) // height
    per = width // height
    for t in range(tiles):
        total = jnp.zeros((height, width), F32)
        for i, (bands, cols, pred) in enumerate(parts):
            total = total + pred[q, t]
            count = bands.shape[3] // strip
            for n in range(n_nb):
                v = mm(cols[q, t], wp[:, n * strip : (n + 1) * strip])
                high, low = split(v)
                for r in range(count):
                    span = slice(r * height, (r + 1) * height)
                    vl[:, r * strip : (r + 1) * strip] = high[span]
                    if i == 0:
                        vn[n, r, 0:height, :] = high[span]
                        vn[n, r, height : 2 * height, :] = low[span]
                total = total + mm(vl[:, : count * strip], bands[q, n, t])
        cut = slice(t * width, (t + 1) * width)
        residual = keep[:, cut] * (total - meas[0, q, :, cut].astype(F32))
        residual = residual.astype(BF).astype(F32)
        turned = jnp.transpose(jnp.concatenate([residual] * per, axis=0)).astype(BF)
        pair = turned[:, : 2 * height]
        x = lax.broadcasted_iota(jnp.int32, (width, strip), 0) + t * width
        j = lax.broadcasted_iota(jnp.int32, (width, strip), 1)
        for r in range(ranks):
            near = mm(pair, v_own[q, t, r])
            far = jnp.zeros((width, strip), F32)
            for n in range(n_nb):
                mask = below(scalars[tiles + n], j, x)
                far = far + jnp.where(mask, mm(pair, vn[n, r]), 0.0)
            i = t * ranks + r
            acc[8 * i : 8 * i + 8, :] = pltpu.roll(
                fold(jnp.concatenate([far, near], axis=1)), lanes - (t * width + 1), 1
            )
            for c in range(tiles * ranks // per):
                hit = block + c * per == i
                spread[i * width : (i + 1) * width, c * width : (c + 1) * width] = jnp.where(
                    hit, turned.astype(F32), 0.0
                ).astype(BF)
    for n in range(n_nb + 1):
        cat = cat_own[q] if n == n_nb else cat_nb[q, n]
        high, low = split(mm(cat, spread[...]))
        us[0, n * strip : (n + 1) * strip, :] = high
        us[1, n * strip : (n + 1) * strip, :] = low
    z = jnp.transpose(mm(wp[...], us[0]) + mm(wp[...], us[1]))
    for i in range(tiles * ranks):
        acc_z[8 * i : 8 * i + 8, :] = fold(z[i * height : (i + 1) * height])
    row_grads = settle(acc[...]) * scale
    col_grads = settle(acc_z[...])[:, :lanes] * scale
    for s in range(tiles):
        row = jnp.zeros((ranks, lanes), F32)
        col = jnp.zeros((ranks, lanes), F32)
        for t in range(tiles):
            hit = scalars[t] == s
            span = slice(t * ranks, (t + 1) * ranks)
            row = row + jnp.where(hit, row_grads[span], 0.0)
            col = col + jnp.where(hit, col_grads[span], 0.0)
        out[0, s] = row
        out[1, s] = col


def body(pattern, measured, row_kernels, col_kernels, tile_patch, sat_tiles):
    _, colours, rows, strip = pattern.shape
    height = measured.shape[2]
    tiles, _, ranks, taps = row_kernels.shape
    width = strip // tiles
    lanes = 2 * strip
    depth = -(-rows // 128) * 128
    fields = lax.axis_size("field")
    banks = lax.axis_size("bank")
    caps = lax.axis_size("cap")
    here = lax.axis_index("field")

    rest = ((0, 0),) * 3 + ((0, lanes - taps),)
    kern = jnp.stack([jnp.flip(jnp.pad(row_kernels, rest), 3), jnp.pad(col_kernels, rest)])

    halos = []
    for q in range(colours):
        part = pattern[:, q : q + 1]
        if fields == 2:
            halos.append([exchange(part, "field", 1)])
        else:
            right = [(i, i + 1) for i in range(fields - 1)]
            left = [(i + 1, i) for i in range(fields - 1)]
            halos.append([lax.ppermute(part, "field", right), lax.ppermute(part, "field", left)])
    sides = [here] if fields == 2 else [jnp.ones_like(here), jnp.zeros_like(here)]
    n_nb = len(sides)
    scalars = jnp.concatenate([tile_patch, jnp.stack(sides).astype(jnp.int32)])

    others = [exchange(kern, "bank", k) for k in range(1, banks)]
    pieces = [[kern], others[:1], others[1:]]

    strip_tiles = strip // TILE
    across = strip_tiles * fields
    row_ids = jnp.arange(height // TILE, dtype=jnp.int32)
    col_ids = here * strip_tiles + jnp.arange(strip_tiles, dtype=jnp.int32)
    tile_ids = row_ids[:, None] * across + col_ids[None, :]
    saturated = jnp.any(tile_ids[:, :, None] == sat_tiles[0][None, None, :], axis=-1)
    keep = 1.0 - saturated.astype(F32)
    keep = jnp.broadcast_to(
        keep[:, None, :, None], (height // TILE, TILE, strip_tiles, TILE)
    ).reshape(height, strip)

    vmem = pltpu.VMEM
    smem = pl.BlockSpec(memory_space=pltpu.SMEM)
    whole = pl.BlockSpec(memory_space=pltpu.VMEM)
    params = pltpu.CompilerParams(vmem_limit_bytes=24 * 2**20)
    cells = tiles * ranks

    fronts = []
    extras = None
    for i, piece in enumerate(pieces):
        own = i == 0
        held = len(piece) * ranks
        shapes = [
            ((colours, n_nb, tiles, held * strip, width), BF),
            ((colours, tiles, held * height, depth), BF),
            ((colours, tiles, height, width), F32),
        ]
        if own:
            shapes += [
                ((colours, strip, cells * width), BF),
                ((colours, n_nb, strip, cells * width), BF),
                ((colours, tiles, ranks, 2 * height, strip), BF),
            ]
        dims = (len(piece), own, colours, n_nb, tiles, width, strip, rows, height, ranks)
        got = pl.pallas_call(
            functools.partial(front, dims),
            in_specs=[smem] + [whole] * (1 + len(piece)),
            out_specs=[whole] * len(shapes),
            out_shape=[jax.ShapeDtypeStruct(s, d) for s, d in shapes],
            scratch_shapes=[
                vmem((depth, strip), BF),
                vmem((held * strip, width), BF),
                vmem((height, held * strip), BF),
                vmem((n_nb, tiles, strip, width), BF),
            ],
            compiler_params=params,
            cost_estimate=pl.CostEstimate(
                flops=2 * 10**8 * len(piece), bytes_accessed=4 * 10**6, transcendentals=0
            ),
            name=f"front{i}",
        )(scalars, pattern, *piece)
        fronts += got[:3]
        if own:
            extras = got[3:]

    grads = []
    for q in range(colours):
        dims = (q, n_nb, len(pieces), tiles, width, strip, rows, height, ranks, 1.0 / height)
        most = max(len(p) for p in pieces) * ranks
        grads.append(
            pl.pallas_call(
                functools.partial(back, dims),
                in_specs=[smem] + [whole] * (3 + n_nb + len(fronts) + len(extras)),
                out_specs=whole,
                out_shape=jax.ShapeDtypeStruct((2, tiles, ranks, lanes), F32),
                scratch_shapes=[
                    vmem((depth, (n_nb + 1) * strip), BF),
                    vmem((height, most * strip), BF),
                    vmem((n_nb, ranks, 2 * height, strip), BF),
                    vmem((cells * width, cells * height), BF),
                    vmem((2, (n_nb + 1) * strip, cells * height), BF),
                    vmem((8 * cells, lanes), F32),
                    vmem((8 * cells, depth), F32),
                ],
                compiler_params=params,
                cost_estimate=pl.CostEstimate(
                    flops=10**9, bytes_accessed=4 * 10**6, transcendentals=0
                ),
                name=f"back{q}",
            )(scalars, pattern, measured, keep, *halos[q], *fronts, *extras)
        )
    grads = jnp.stack(grads, axis=2)
    step = caps // 2
    while step:
        grads = grads + exchange(grads, "cap", step)
        step //= 2
    grads = grads[..., :taps]
    return grads[0], grads[1]


def solution(mesh):
    return jax.shard_map(
        body,
        mesh=mesh,
        in_specs=(
            P("cap", None, None, "field"),
            P("cap", None, None, "field"),
            P("field", None, "bank", None),
            P("field", None, "bank", None),
            P("field"),
            P("cap", None),
        ),
        out_specs=(P("field", None, "bank", None), P("field", None, "bank", None)),
        check_vma=False,
    )
```

```python
import functools

import jax
import jax.numpy as jnp
from jax import lax
from jax.experimental import pallas as pl
from jax.experimental.pallas import tpu as pltpu
from jax.sharding import PartitionSpec as P

TILE = 16
BF = jnp.bfloat16
F32 = jnp.float32


def mm(a, b):
    return jnp.dot(a, b, preferred_element_type=F32)


def mt(a, b):
    return lax.dot_general(a, b, (((1,), (1,)), ((), ())), preferred_element_type=F32)


def split(v):
    high = v.astype(BF)
    return high, (v - high.astype(F32)).astype(BF)


def exchange(cells, axis, step):
    count = lax.axis_size(axis)
    return lax.ppermute(cells, axis, [(i, i ^ step) for i in range(count)])


def fill(dst, at, cells):
    rows, width = cells.shape
    depth = dst.shape[0]
    whole = rows // 16 * 16
    dst[whole:depth, at : at + width] = jnp.zeros((depth - whole, width), BF)
    dst[0:rows, at : at + width] = cells


def below(side, j, x):
    left = (j > x).astype(jnp.int32)
    right = (j < x).astype(jnp.int32)
    return (side * left + (1 - side) * right) > 0


def front(dims, scalars, w_ref, *refs):
    count, colours, n_nb, tiles, width, strip, rows, height, ranks = dims
    kern = refs[:count]
    band_nb, band_own, cols, v_own, pred, wp, vl, masks = refs[count:]
    lanes = 2 * strip
    depth = wp.shape[0]
    held = count * ranks
    for n in range(n_nb):
        for t in range(tiles):
            x = lax.broadcasted_iota(jnp.int32, (width, strip), 0) + t * width
            j = lax.broadcasted_iota(jnp.int32, (width, strip), 1)
            masks[n, t] = below(scalars[tiles + n], j, x).astype(F32).astype(BF)

    @pl.loop(0, colours)
    def _(q):
        fill(wp, 0, w_ref[0, q])
        for t in range(tiles):
            pick = scalars[t]
            for p in range(count):
                taps = kern[p][1, pick, q].astype(F32)
                taps = jnp.concatenate([taps, jnp.zeros((ranks, depth - lanes), F32)], axis=1)
                for r in range(ranks):
                    first = (p * ranks + r) * height
                    one = jnp.broadcast_to(taps[r : r + 1], (height, depth)).astype(BF)
                    cols[q, t, first : first + height, :] = pltpu.roll(
                        one, 0, 1, stride=1, stride_axis=0
                    )
            v = mm(cols[q, t], wp[...])
            vl[t] = v.astype(BF)
            for r in range(ranks):
                high, low = split(v[r * height : (r + 1) * height])
                v_own[q, t, r, 0:height, :] = high
                v_own[q, t, r, height : 2 * height, :] = low
        for t in range(tiles):
            pick = scalars[t]
            total = jnp.zeros((height, width), F32)
            for p in range(count):
                taps = kern[p][0, pick, q].astype(F32)
                for r in range(ranks):
                    slot = p * ranks + r
                    at = slot * strip
                    one = jnp.broadcast_to(taps[r : r + 1], (width, lanes)).astype(BF)
                    tile = pltpu.roll(one, 1 + t * width, 1, stride=1, stride_axis=0)
                    for n in range(n_nb):
                        band_nb[q, n, t, :, at : at + strip] = tile[:, :strip] * masks[n, t]
                    if p == 0:
                        band_own[q, t, :, at : at + strip] = tile[:, strip:]
                    total = total + mt(
                        vl[t, slot * height : (slot + 1) * height, :], tile[:, strip:]
                    )
            pred[q, t] = total


def fold(rows):
    lanes = rows.shape[1]
    total = rows[0:8]
    for g in range(1, rows.shape[0] // 8):
        total = total + pltpu.roll(rows[8 * g : 8 * g + 8], lanes - 8 * g, 1)
    return total


def settle(acc):
    blocks, count, wide = acc.shape
    total = None
    for i in reversed(range(8)):
        rows = jnp.concatenate(
            [acc[c, pl.ds(i, count // 8, stride=8), :] for c in range(blocks)], axis=1
        )
        if total is None:
            total = rows
        else:
            total = pltpu.roll(total, blocks * wide - 1, 1) + rows
    return total


def keep_in(acc, first, rows):
    for c in range(acc.shape[0]):
        acc[c, first : first + rows.shape[0], :] = rows[:, c * 128 : (c + 1) * 128]


def back(dims, scalars, w_own, meas, keep, *refs):
    q, n_nb, held, tiles, width, strip, rows, height, ranks, scale = dims
    halos = refs[:n_nb]
    band_nb, band_own, cols, v_own, pred, out, wp, vl, vn, us, acc, acc_z = refs[n_nb:]
    lanes = 2 * strip
    near = ranks * strip
    cells = tiles * ranks
    for n in range(n_nb):
        fill(wp, n * strip, halos[n][0, 0])
    fill(wp, n_nb * strip, w_own[0, q])
    for n in range(n_nb):
        for t in range(tiles):
            v = mm(cols[q, t], wp[:, n * strip : (n + 1) * strip])
            vl[n, t] = v.astype(BF)
            for r in range(ranks):
                high, low = split(v[r * height : (r + 1) * height])
                vn[n, t, r, 0:height, :] = high
                vn[n, t, r, height : 2 * height, :] = low
    for t in range(tiles):
        total = pred[q, t]
        for n in range(n_nb):
            for r in range(held):
                total = total + mt(
                    vl[n, t, r * height : (r + 1) * height, :],
                    band_nb[q, n, t, :, r * strip : (r + 1) * strip],
                )
        cut = slice(t * width, (t + 1) * width)
        residual = keep[:, cut] * (total - meas[0, q, :, cut].astype(F32))
        residual = residual.astype(BF)
        wide = residual.astype(F32)
        pair = jnp.transpose(jnp.concatenate([wide] * (width // height), axis=0)).astype(BF)
        pair = pair[:, : 2 * height]
        x = lax.broadcasted_iota(jnp.int32, (width, strip), 0) + t * width
        j = lax.broadcasted_iota(jnp.int32, (width, strip), 1)
        for n in range(n_nb + 1):
            bands = band_own[q, t] if n == n_nb else band_nb[q, n, t, :, :near]
            high, low = split(mm(residual, bands))
            for r in range(ranks):
                first = (t * ranks + r) * height
                take = slice(r * strip, (r + 1) * strip)
                span = slice(n * strip, (n + 1) * strip)
                us[first : first + height, span] = high[:, take]
                us[cells * height + first : cells * height + first + height, span] = low[:, take]
        for r in range(ranks):
            far = jnp.zeros((width, strip), F32)
            for n in range(n_nb):
                mask = below(scalars[tiles + n], j, x)
                far = far + jnp.where(mask, mm(pair, vn[n, t, r]), 0.0)
            both = jnp.concatenate([far, mm(pair, v_own[q, t, r])], axis=1)
            part = pltpu.roll(fold(both), lanes - (t * width + 1), 1)
            keep_in(acc, 8 * (t * ranks + r), part)
    z = mt(us[...], wp[...])
    z = z[: cells * height] + z[cells * height :]
    for i in range(cells):
        keep_in(acc_z, 8 * i, fold(z[i * height : (i + 1) * height]))
    row_grads = settle(acc) * scale
    col_grads = settle(acc_z)[:, :lanes] * scale
    for s in range(tiles):
        row = jnp.zeros((ranks, lanes), F32)
        col = jnp.zeros((ranks, lanes), F32)
        for t in range(tiles):
            hit = scalars[t] == s
            span = slice(t * ranks, (t + 1) * ranks)
            row = row + jnp.where(hit, row_grads[span], 0.0)
            col = col + jnp.where(hit, col_grads[span], 0.0)
        out[0, s] = row
        out[1, s] = col


def body(pattern, measured, row_kernels, col_kernels, tile_patch, sat_tiles):
    _, colours, rows, strip = pattern.shape
    height = measured.shape[2]
    tiles, _, ranks, taps = row_kernels.shape
    width = strip // tiles
    lanes = 2 * strip
    depth = -(-rows // 128) * 128
    fields = lax.axis_size("field")
    banks = lax.axis_size("bank")
    caps = lax.axis_size("cap")
    here = lax.axis_index("field")

    rest = ((0, 0),) * 3 + ((0, lanes - taps),)
    kern = jnp.pad(jnp.stack([row_kernels, col_kernels]), ((0, 0),) + rest)

    halos = []
    for q in range(colours):
        part = pattern[:, q : q + 1]
        if fields == 2:
            halos.append([exchange(part, "field", 1)])
        else:
            right = [(i, i + 1) for i in range(fields - 1)]
            left = [(i + 1, i) for i in range(fields - 1)]
            halos.append([lax.ppermute(part, "field", right), lax.ppermute(part, "field", left)])
    sides = [here] if fields == 2 else [jnp.ones_like(here), jnp.zeros_like(here)]
    n_nb = len(sides)
    scalars = jnp.concatenate([tile_patch, jnp.stack(sides).astype(jnp.int32)])

    pieces = [kern] + [exchange(kern, "bank", k) for k in range(1, banks)]

    strip_tiles = strip // TILE
    across = strip_tiles * fields
    row_ids = jnp.arange(height // TILE, dtype=jnp.int32)
    col_ids = here * strip_tiles + jnp.arange(strip_tiles, dtype=jnp.int32)
    tile_ids = row_ids[:, None] * across + col_ids[None, :]
    saturated = jnp.any(tile_ids[:, :, None] == sat_tiles[0][None, None, :], axis=-1)
    keep = 1.0 - saturated.astype(F32)
    keep = jnp.broadcast_to(
        keep[:, None, :, None], (height // TILE, TILE, strip_tiles, TILE)
    ).reshape(height, strip)

    vmem = pltpu.VMEM
    smem = pl.BlockSpec(memory_space=pltpu.SMEM)
    whole = pl.BlockSpec(memory_space=pltpu.VMEM)
    params = pltpu.CompilerParams(vmem_limit_bytes=24 * 2**20)
    cells = tiles * ranks

    held = len(pieces) * ranks
    shapes = [
        ((colours, n_nb, tiles, width, held * strip), BF),
        ((colours, tiles, width, ranks * strip), BF),
        ((colours, tiles, held * height, depth), BF),
        ((colours, tiles, ranks, 2 * height, strip), BF),
        ((colours, tiles, height, width), F32),
    ]
    fronts = pl.pallas_call(
        functools.partial(
            front, (len(pieces), colours, n_nb, tiles, width, strip, rows, height, ranks)
        ),
        in_specs=[smem] + [whole] * (1 + len(pieces)),
        out_specs=[whole] * len(shapes),
        out_shape=[jax.ShapeDtypeStruct(s, d) for s, d in shapes],
        scratch_shapes=[
            vmem((depth, strip), BF),
            vmem((tiles, held * height, strip), BF),
            vmem((n_nb, tiles, width, strip), BF),
        ],
        compiler_params=params,
        cost_estimate=pl.CostEstimate(
            flops=2 * 10**9, bytes_accessed=4 * 10**6, transcendentals=0
        ),
        name="front",
    )(scalars, pattern, *pieces)

    grads = []
    for q in range(colours):
        dims = (q, n_nb, held, tiles, width, strip, rows, height, ranks, 1.0 / height)
        grads.append(
            pl.pallas_call(
                functools.partial(back, dims),
                in_specs=[smem] + [whole] * (3 + n_nb + len(fronts)),
                out_specs=whole,
                out_shape=jax.ShapeDtypeStruct((2, tiles, ranks, lanes), F32),
                scratch_shapes=[
                    vmem((depth, (n_nb + 1) * strip), BF),
                    vmem((n_nb, tiles, held * height, strip), BF),
                    vmem((n_nb, tiles, ranks, 2 * height, strip), BF),
                    vmem((2 * cells * height, (n_nb + 1) * strip), BF),
                    vmem((lanes // 128, 8 * cells, 128), F32),
                    vmem((depth // 128, 8 * cells, 128), F32),
                ],
                compiler_params=params,
                cost_estimate=pl.CostEstimate(
                    flops=10**9, bytes_accessed=4 * 10**6, transcendentals=0
                ),
                name=f"back{q}",
            )(scalars, pattern, measured, keep, *halos[q], *fronts)
        )
    grads = jnp.stack(grads, axis=2)
    step = caps // 2
    while step:
        grads = grads + exchange(grads, "cap", step)
        step //= 2
    grads = grads[..., :taps]
    return grads[0], grads[1]


def solution(mesh):
    return jax.shard_map(
        body,
        mesh=mesh,
        in_specs=(
            P("cap", None, None, "field"),
            P("cap", None, None, "field"),
            P("field", None, "bank", None),
            P("field", None, "bank", None),
            P("field"),
            P("cap", None),
        ),
        out_specs=(P("field", None, "bank", None), P("field", None, "bank", None)),
        check_vma=False,
    )
```

```python
import functools

import jax
import jax.numpy as jnp
from jax import lax
from jax.experimental import pallas as pl
from jax.experimental.pallas import tpu as pltpu
from jax.sharding import PartitionSpec as P

TILE = 16
BF = jnp.bfloat16
F32 = jnp.float32


def mm(a, b):
    return jnp.dot(a, b, preferred_element_type=F32)


def mt(a, b):
    return lax.dot_general(a, b, (((1,), (1,)), ((), ())), preferred_element_type=F32)


def split(v):
    high = v.astype(BF)
    return high, (v - high.astype(F32)).astype(BF)


def exchange(cells, axis, step):
    count = lax.axis_size(axis)
    return lax.ppermute(cells, axis, [(i, i ^ step) for i in range(count)])


def fill(dst, at, cells):
    rows, width = cells.shape
    depth = dst.shape[0]
    whole = rows // 16 * 16
    dst[whole:depth, at : at + width] = jnp.zeros((depth - whole, width), BF)
    dst[0:rows, at : at + width] = cells


def below(side, j, x):
    left = (j > x).astype(jnp.int32)
    right = (j < x).astype(jnp.int32)
    return (side * left + (1 - side) * right) > 0


def side_of(n, n_nb, here):
    return here if n_nb == 1 else jnp.int32(1 - n)


def prep(pattern, measured, sat_tiles, row_kernels, col_kernels, *refs):
    colours = pattern.shape[1]
    strips = refs[:colours]
    kern, meas, sat, rows_in, cols_in, rows, cols, sems = refs[colours:]
    tiles, _, ranks, taps = row_kernels.shape
    lanes = rows.shape[1]
    pairs = [(row_kernels, rows_in), (col_kernels, cols_in)]
    pairs += [(pattern.at[:, pl.ds(q, 1)], strips[q]) for q in range(colours)]
    pairs += [(sat_tiles, sat), (measured, meas)]
    copies = [pltpu.make_async_copy(a, b, sems.at[i]) for i, (a, b) in enumerate(pairs)]
    for copy in copies:
        copy.start()
    rows[...] = jnp.zeros(rows.shape, F32)
    cols[...] = jnp.zeros(cols.shape, F32)
    i = lax.broadcasted_iota(jnp.int32, (lanes, lanes), 0)
    m = lax.broadcasted_iota(jnp.int32, (lanes, lanes), 1)
    mirror = (i + m == lanes - 1).astype(F32).astype(BF)
    copies[0].wait()
    copies[1].wait()
    for s in range(tiles):
        for q in range(colours):
            first = (s * colours + q) * ranks
            rows[first : first + ranks, 0:taps] = rows_in[s, q].astype(F32)
            cols[first : first + ranks, 0:taps] = cols_in[s, q].astype(F32)
    mirrored = mm(rows[...].astype(BF), mirror)
    for s in range(tiles):
        for q in range(colours):
            first = (s * colours + q) * ranks
            kern[0, s, q] = mirrored[first : first + ranks].astype(BF)
            kern[1, s, q] = cols[first : first + ranks, :].astype(BF)
    for copy in copies[2:]:
        copy.wait()


def front(dims, tile_patch, sat, *refs):
    count, own, colours, n_nb, tiles, width, strip, rows, height, ranks, fields = dims
    strips = refs[:colours]
    kern = refs[colours : colours + count]
    band_nb, cols, pred = refs[colours + count : colours + count + 3]
    if own:
        band_own, v_own, keep = refs[colours + count + 3 : -5]
    wp, vl, masks, picks, sem = refs[-5:]
    fetch = pltpu.make_async_copy(tile_patch, picks, sem)
    fetch.start()
    lanes = 2 * strip
    depth = wp.shape[0]
    here = lax.axis_index("field")
    for n in range(n_nb):
        side = side_of(n, n_nb, here)
        for t in range(tiles):
            j = lax.broadcasted_iota(jnp.int32, (strip, width), 0)
            x = lax.broadcasted_iota(jnp.int32, (strip, width), 1) + t * width
            masks[n, t] = below(side, j, x).astype(F32).astype(BF)
    if own:
        across = strip // TILE
        boxes = height // TILE * across
        box = lax.broadcasted_iota(jnp.int32, (boxes, 1), 0)
        name = box // across * (across * fields) + here * across + box % across
        hit = jnp.max((sat[...] == name).astype(F32), axis=1, keepdims=True)
        x = lax.broadcasted_iota(jnp.int32, (boxes, strip), 1) // TILE
        wide = jnp.where(x == box % across, hit, 0.0).astype(BF)
        y = lax.broadcasted_iota(jnp.int32, (height, boxes), 0) // TILE
        tall = y == lax.broadcasted_iota(jnp.int32, (height, boxes), 1) // across
        keep[...] = 1.0 - mm(tall.astype(F32).astype(BF), wide)
    fetch.wait()

    for q in range(colours):
        fill(wp, 0, strips[q][0, 0])
        for t in range(tiles):
            pick = picks[t]
            for p in range(count):
                taps = kern[p][1, pick, q].astype(F32)
                taps = jnp.concatenate([taps, jnp.zeros((ranks, depth - lanes), F32)], axis=1)
                for r in range(ranks):
                    first = (p * ranks + r) * height
                    one = jnp.broadcast_to(taps[r : r + 1], (height, depth)).astype(BF)
                    cols[q, t, first : first + height, :] = pltpu.roll(
                        one, 0, 1, stride=1, stride_axis=0
                    )
            v = mm(cols[q, t], wp[...])
            vl[t] = v.astype(BF)
            for r in range(ranks if own else 0):
                high, low = split(v[r * height : (r + 1) * height])
                v_own[q, t, r, 0:height, :] = high
                v_own[q, t, r, height : 2 * height, :] = low
        for t in range(tiles):
            pick = picks[t]
            total = jnp.zeros((height, width), F32)
            for p in range(count):
                taps = kern[p][0, pick, q].astype(F32)
                for r in range(ranks):
                    slot = p * ranks + r
                    at = slot * strip
                    one = jnp.broadcast_to(taps[r : r + 1], (width, lanes)).astype(BF)
                    base = pltpu.roll(one, 0, 1, stride=1, stride_axis=0)
                    blocks = []
                    for a in range(lanes // width):
                        first = (t - a) % (lanes // width) * width
                        blocks.append(base[:, first : first + width])
                    half = len(blocks) // 2
                    for a in range(half):
                        span = slice(a * width, (a + 1) * width)
                        for n in range(n_nb):
                            band_nb[q, n, t, at + a * width : at + (a + 1) * width, :] = (
                                blocks[a] * masks[n, t, span, :]
                            )
                    rest = jnp.concatenate(blocks[half:], axis=0)
                    if own and p == 0:
                        band_own[q, t, at : at + strip, :] = rest
                    total = total + mm(vl[t, slot * height : (slot + 1) * height, :], rest)
            pred[q, t] = total


def fold(rows):
    lanes = rows.shape[1]
    total = rows[0:8]
    for g in range(1, rows.shape[0] // 8):
        total = total + pltpu.roll(rows[8 * g : 8 * g + 8], lanes - 8 * g, 1)
    return total


def settle(acc):
    blocks, count, wide = acc.shape
    total = None
    for i in reversed(range(8)):
        rows = jnp.concatenate(
            [acc[c, pl.ds(i, count // 8, stride=8), :] for c in range(blocks)], axis=1
        )
        if total is None:
            total = rows
        else:
            total = pltpu.roll(total, blocks * wide - 1, 1) + rows
    return total


def keep_in(acc, first, rows):
    for c in range(acc.shape[0]):
        acc[c, first : first + rows.shape[0], :] = rows[:, c * 128 : (c + 1) * 128]


def back(dims, tile_patch, w_own, meas, keep, *refs):
    q, n_nb, parts, tiles, width, strip, rows, height, ranks, scale = dims
    halos = refs[:n_nb]
    fronts = [refs[n_nb + 3 * i : n_nb + 3 * i + 3] for i in range(parts)]
    band_own, v_own, out, wp, vl, vn, us, acc, acc_z, picks, sem = refs[n_nb + 3 * parts :]
    fetch = pltpu.make_async_copy(tile_patch, picks, sem)
    fetch.start()
    lanes = 2 * strip
    near = ranks * strip
    cells = tiles * ranks
    here = lax.axis_index("field")
    for n in range(n_nb):
        fill(wp, n * strip, halos[n][0, 0])
    fill(wp, n_nb * strip, w_own[0, 0])
    for n in range(n_nb):
        for t in range(tiles):
            first = 0
            for i, (_, cols, _) in enumerate(fronts):
                v = mm(cols[q, t], wp[:, n * strip : (n + 1) * strip])
                vl[n, t, first : first + v.shape[0]] = v.astype(BF)
                first += v.shape[0]
                for r in range(ranks if i == 0 else 0):
                    high, low = split(v[r * height : (r + 1) * height])
                    vn[n, t, r, 0:height, :] = high
                    vn[n, t, r, height : 2 * height, :] = low
    pairs = []
    for t in range(tiles):
        total = jnp.zeros((height, width), F32)
        first = 0
        for bands, _, pred in fronts:
            total = total + pred[q, t]
            for r in range(bands.shape[3] // strip):
                for n in range(n_nb):
                    total = total + mm(
                        vl[n, t, first : first + height, :],
                        bands[q, n, t, r * strip : (r + 1) * strip, :],
                    )
                first += height
        cut = slice(t * width, (t + 1) * width)
        residual = keep[:, cut] * (total - meas[0, q, :, cut].astype(F32))
        residual = residual.astype(BF)
        wide = residual.astype(F32)
        pair = jnp.transpose(jnp.concatenate([wide] * (width // height), axis=0)).astype(BF)
        pairs.append(pair[:, : 2 * height])
        for n in range(n_nb + 1):
            bands = band_own[q, t] if n == n_nb else fronts[0][0][q, n, t, :near, :]
            high, low = split(mt(residual, bands))
            for r in range(ranks):
                first = (t * ranks + r) * height
                take = slice(r * strip, (r + 1) * strip)
                span = slice(n * strip, (n + 1) * strip)
                us[first : first + height, span] = high[:, take]
                us[cells * height + first : cells * height + first + height, span] = low[:, take]
    z = mt(us[...], wp[...])
    z = z[: cells * height] + z[cells * height :]
    for t in range(tiles):
        x = lax.broadcasted_iota(jnp.int32, (width, strip), 0) + t * width
        j = lax.broadcasted_iota(jnp.int32, (width, strip), 1)
        for r in range(ranks):
            far = jnp.zeros((width, strip), F32)
            for n in range(n_nb):
                mask = below(side_of(n, n_nb, here), j, x)
                far = far + jnp.where(mask, mm(pairs[t], vn[n, t, r]), 0.0)
            both = jnp.concatenate([far, mm(pairs[t], v_own[q, t, r])], axis=1)
            part = pltpu.roll(fold(both), lanes - (t * width + 1), 1)
            keep_in(acc, 8 * (t * ranks + r), part)
    for i in range(cells):
        keep_in(acc_z, 8 * i, fold(z[i * height : (i + 1) * height]))
    fetch.wait()
    row_grads = settle(acc) * scale
    col_grads = settle(acc_z)[:, :lanes] * scale
    for s in range(tiles):
        row = jnp.zeros((ranks, lanes), F32)
        col = jnp.zeros((ranks, lanes), F32)
        for t in range(tiles):
            hit = picks[t] == s
            span = slice(t * ranks, (t + 1) * ranks)
            row = row + jnp.where(hit, row_grads[span], 0.0)
            col = col + jnp.where(hit, col_grads[span], 0.0)
        out[0, s] = row
        out[1, s] = col


def finish(mine, theirs, rows, cols):
    taps = rows.shape[-1]
    for s in range(rows.shape[0]):
        for q in range(rows.shape[1]):
            rows[s, q] = (mine[0, s, q] + theirs[0, s, q])[:, :taps]
            cols[s, q] = (mine[1, s, q] + theirs[1, s, q])[:, :taps]


def body(pattern, measured, row_kernels, col_kernels, tile_patch, sat_tiles):
    _, colours, rows, strip = pattern.shape
    height = measured.shape[2]
    tiles, _, ranks, taps = row_kernels.shape
    width = strip // tiles
    lanes = 2 * strip
    depth = -(-rows // 128) * 128
    fields = lax.axis_size("field")
    banks = lax.axis_size("bank")
    caps = lax.axis_size("cap")
    cells = tiles * ranks

    vmem = pltpu.VMEM
    hbm = pl.BlockSpec(memory_space=pltpu.HBM)
    whole = pl.BlockSpec(memory_space=pltpu.VMEM)
    params = pltpu.CompilerParams(vmem_limit_bytes=24 * 2**20)

    def cost(flops):
        return pl.CostEstimate(flops=flops, bytes_accessed=4 * 10**6, transcendentals=0)

    pattern, measured, row_kernels, col_kernels, tile_patch, sat_tiles = [
        pltpu.with_memory_space_constraint(array, pltpu.HBM)
        for array in (pattern, measured, row_kernels, col_kernels, tile_patch, sat_tiles)
    ]
    *strips, kern, meas, sat = pl.pallas_call(
        prep,
        in_specs=[hbm] * 5,
        out_specs=[whole] * (colours + 3),
        out_shape=[jax.ShapeDtypeStruct((1, 1, rows, strip), BF)] * colours
        + [
            jax.ShapeDtypeStruct((2, tiles, colours, ranks, lanes), BF),
            jax.ShapeDtypeStruct(measured.shape, measured.dtype),
            jax.ShapeDtypeStruct(sat_tiles.shape, sat_tiles.dtype),
        ],
        scratch_shapes=[
            vmem(row_kernels.shape, BF),
            vmem(col_kernels.shape, BF),
            vmem((tiles * colours * ranks, lanes), F32),
            vmem((tiles * colours * ranks, lanes), F32),
            pltpu.SemaphoreType.DMA((colours + 4,)),
        ],
        compiler_params=params,
        cost_estimate=cost(10**7),
        name="prep",
    )(pattern, measured, sat_tiles, row_kernels, col_kernels)

    halos = []
    for part in strips:
        if fields == 2:
            halos.append([exchange(part, "field", 1)])
        else:
            right = [(i, i + 1) for i in range(fields - 1)]
            left = [(i + 1, i) for i in range(fields - 1)]
            halos.append([lax.ppermute(part, "field", right), lax.ppermute(part, "field", left)])
    n_nb = len(halos[0])
    pieces = [kern] + [exchange(kern, "bank", k) for k in range(1, banks)]
    held = len(pieces) * ranks

    own_shapes = [
        ((colours, tiles, ranks * strip, width), BF),
        ((colours, tiles, ranks, 2 * height, strip), BF),
        ((height, strip), F32),
    ]
    cuts = [pieces[:2], pieces[2:]]
    fronts = []
    for i, cut in enumerate(cuts):
        some = len(cut) * ranks
        shapes = [
            ((colours, n_nb, tiles, some * strip, width), BF),
            ((colours, tiles, some * height, depth), BF),
            ((colours, tiles, height, width), F32),
        ]
        if i == 0:
            shapes += own_shapes
        dims = (len(cut), i == 0, colours, n_nb, tiles, width, strip, rows, height, ranks, fields)
        got = pl.pallas_call(
            functools.partial(front, dims),
            in_specs=[hbm] + [whole] * (1 + colours + len(cut)),
            out_specs=[whole] * len(shapes),
            out_shape=[jax.ShapeDtypeStruct(s, d) for s, d in shapes],
            scratch_shapes=[
                vmem((depth, strip), BF),
                vmem((tiles, some * height, strip), BF),
                vmem((n_nb, tiles, strip, width), BF),
                pltpu.SMEM((tiles,), jnp.int32),
                pltpu.SemaphoreType.DMA,
            ],
            compiler_params=params,
            cost_estimate=cost(10**9),
            name=f"front{i}",
        )(tile_patch, sat, *strips, *cut)
        fronts += got[:3]
        if i == 0:
            band_own, v_own, keep = got[3:]

    grads = []
    for q in range(colours):
        dims = (q, n_nb, len(cuts), tiles, width, strip, rows, height, ranks, 1.0 / height)
        grads.append(
            pl.pallas_call(
                functools.partial(back, dims),
                in_specs=[hbm] + [whole] * (5 + n_nb + len(fronts)),
                out_specs=whole,
                out_shape=jax.ShapeDtypeStruct((2, tiles, ranks, lanes), F32),
                scratch_shapes=[
                    vmem((depth, (n_nb + 1) * strip), BF),
                    vmem((n_nb, tiles, held * height, strip), BF),
                    vmem((n_nb, tiles, ranks, 2 * height, strip), BF),
                    vmem((2 * cells * height, (n_nb + 1) * strip), BF),
                    vmem((lanes // 128, 8 * cells, 128), F32),
                    vmem((depth // 128, 8 * cells, 128), F32),
                    pltpu.SMEM((tiles,), jnp.int32),
                    pltpu.SemaphoreType.DMA,
                ],
                compiler_params=params,
                cost_estimate=cost(10**9),
                name=f"back{q}",
            )(tile_patch, strips[q], meas, keep, *halos[q], *fronts, band_own, v_own)
        )
    grads = jnp.stack(grads, axis=2)
    step = caps // 2
    while step > 1:
        grads = grads + exchange(grads, "cap", step)
        step //= 2
    out = jax.ShapeDtypeStruct((tiles, colours, ranks, taps), F32)
    return pl.pallas_call(
        finish,
        in_specs=[whole] * 2,
        out_specs=[whole] * 2,
        out_shape=[out, out],
        compiler_params=params,
        name="finish",
    )(grads, exchange(grads, "cap", 1))


def solution(mesh):
    return jax.shard_map(
        body,
        mesh=mesh,
        in_specs=(
            P("cap", None, None, "field"),
            P("cap", None, None, "field"),
            P("field", None, "bank", None),
            P("field", None, "bank", None),
            P("field"),
            P("cap", None),
        ),
        out_specs=(P("field", None, "bank", None), P("field", None, "bank", None)),
        check_vma=False,
    )
```

```python
import functools

import jax
import jax.numpy as jnp
from jax import lax
from jax.experimental import pallas as pl
from jax.experimental.pallas import tpu as pltpu
from jax.sharding import PartitionSpec as P

TILE = 16
BF = jnp.bfloat16
F32 = jnp.float32


def mm(a, b):
    return jnp.dot(a, b, preferred_element_type=F32)


def mt(a, b):
    return lax.dot_general(a, b, (((1,), (1,)), ((), ())), preferred_element_type=F32)


def split(v):
    high = v.astype(BF)
    return high, (v - high.astype(F32)).astype(BF)


def exchange(cells, axis, step):
    count = lax.axis_size(axis)
    return lax.ppermute(cells, axis, [(i, i ^ step) for i in range(count)])


def fill(dst, at, cells):
    rows, width = cells.shape
    depth = dst.shape[0]
    whole = rows // 16 * 16
    dst[whole:depth, at : at + width] = jnp.zeros((depth - whole, width), BF)
    dst[0:rows, at : at + width] = cells


def below(side, j, x):
    left = (j > x).astype(jnp.int32)
    right = (j < x).astype(jnp.int32)
    return (side * left + (1 - side) * right) > 0


def side_of(n, n_nb, here):
    return here if n_nb == 1 else jnp.int32(1 - n)


def prep(pattern, measured, sat_tiles, row_kernels, col_kernels, *refs):
    colours = pattern.shape[1]
    strips = refs[:colours]
    kern, meas, sat, rows_in, cols_in, rows, cols, sems = refs[colours:]
    tiles, _, ranks, taps = row_kernels.shape
    lanes = rows.shape[1]
    pairs = [(row_kernels, rows_in), (col_kernels, cols_in)]
    pairs += [(pattern.at[:, pl.ds(q, 1)], strips[q]) for q in range(colours)]
    pairs += [(sat_tiles, sat), (measured, meas)]
    copies = [pltpu.make_async_copy(a, b, sems.at[i]) for i, (a, b) in enumerate(pairs)]
    for copy in copies:
        copy.start()
    rows[...] = jnp.zeros(rows.shape, F32)
    cols[...] = jnp.zeros(cols.shape, F32)
    i = lax.broadcasted_iota(jnp.int32, (lanes, lanes), 0)
    m = lax.broadcasted_iota(jnp.int32, (lanes, lanes), 1)
    mirror = (i + m == lanes - 1).astype(F32).astype(BF)
    copies[0].wait()
    copies[1].wait()
    for s in range(tiles):
        for q in range(colours):
            first = (s * colours + q) * ranks
            rows[first : first + ranks, 0:taps] = rows_in[s, q].astype(F32)
            cols[first : first + ranks, 0:taps] = cols_in[s, q].astype(F32)
    mirrored = mm(rows[...].astype(BF), mirror)
    for s in range(tiles):
        for q in range(colours):
            first = (s * colours + q) * ranks
            kern[0, s, q] = mirrored[first : first + ranks].astype(BF)
            kern[1, s, q] = cols[first : first + ranks, :].astype(BF)
    for copy in copies[2:]:
        copy.wait()


def front(dims, tile_patch, sat, *refs):
    count, own, colours, n_nb, tiles, width, strip, rows, height, ranks, fields = dims
    strips = refs[:colours]
    kern = refs[colours : colours + count]
    band_nb, cols, pred = refs[colours + count : colours + count + 3]
    if own:
        band_own, v_own, keep = refs[colours + count + 3 : -5]
    wp, vl, masks, picks, sem = refs[-5:]
    fetch = pltpu.make_async_copy(tile_patch, picks, sem)
    fetch.start()
    lanes = 2 * strip
    depth = wp.shape[0]
    here = lax.axis_index("field")
    for n in range(n_nb):
        side = side_of(n, n_nb, here)
        for t in range(tiles):
            j = lax.broadcasted_iota(jnp.int32, (strip, width), 0)
            x = lax.broadcasted_iota(jnp.int32, (strip, width), 1) + t * width
            masks[n, t] = below(side, j, x).astype(F32).astype(BF)
    if own:
        across = strip // TILE
        boxes = height // TILE * across
        box = lax.broadcasted_iota(jnp.int32, (boxes, 1), 0)
        name = box // across * (across * fields) + here * across + box % across
        hit = jnp.max((sat[...] == name).astype(F32), axis=1, keepdims=True)
        x = lax.broadcasted_iota(jnp.int32, (boxes, strip), 1) // TILE
        wide = jnp.where(x == box % across, hit, 0.0).astype(BF)
        y = lax.broadcasted_iota(jnp.int32, (height, boxes), 0) // TILE
        tall = y == lax.broadcasted_iota(jnp.int32, (height, boxes), 1) // across
        keep[...] = 1.0 - mm(tall.astype(F32).astype(BF), wide)
    fetch.wait()

    for q in range(colours):
        fill(wp, 0, strips[q][0, 0])
        for t in range(tiles):
            pick = picks[t]
            for p in range(count):
                taps = kern[p][1, pick, q].astype(F32)
                taps = jnp.concatenate([taps, jnp.zeros((ranks, depth - lanes), F32)], axis=1)
                for r in range(ranks):
                    first = (p * ranks + r) * height
                    one = jnp.broadcast_to(taps[r : r + 1], (height, depth)).astype(BF)
                    cols[q, t, first : first + height, :] = pltpu.roll(
                        one, 0, 1, stride=1, stride_axis=0
                    )
            v = mm(cols[q, t], wp[...])
            vl[t] = v.astype(BF)
            for r in range(ranks if own else 0):
                high, low = split(v[r * height : (r + 1) * height])
                v_own[q, t, r, 0:height, :] = high
                v_own[q, t, r, height : 2 * height, :] = low
        for t in range(tiles):
            pick = picks[t]
            total = jnp.zeros((height, width), F32)
            for p in range(count):
                taps = kern[p][0, pick, q].astype(F32)
                for r in range(ranks):
                    slot = p * ranks + r
                    at = slot * strip
                    one = jnp.broadcast_to(taps[r : r + 1], (width, lanes)).astype(BF)
                    base = pltpu.roll(one, 0, 1, stride=1, stride_axis=0)
                    blocks = []
                    for a in range(lanes // width):
                        first = (t - a) % (lanes // width) * width
                        blocks.append(base[:, first : first + width])
                    half = len(blocks) // 2
                    for a in range(half):
                        span = slice(a * width, (a + 1) * width)
                        for n in range(n_nb):
                            band_nb[q, n, t, at + a * width : at + (a + 1) * width, :] = (
                                blocks[a] * masks[n, t, span, :]
                            )
                    rest = jnp.concatenate(blocks[half:], axis=0)
                    if own and p == 0:
                        band_own[q, t, at : at + strip, :] = rest
                    total = total + mm(vl[t, slot * height : (slot + 1) * height, :], rest)
            pred[q, t] = total


def fold(rows):
    lanes = rows.shape[1]
    total = rows[0:8]
    for g in range(1, rows.shape[0] // 8):
        total = total + pltpu.roll(rows[8 * g : 8 * g + 8], lanes - 8 * g, 1)
    return total


def settle(acc):
    blocks, count, wide = acc.shape
    total = None
    for i in reversed(range(8)):
        rows = jnp.concatenate(
            [acc[c, pl.ds(i, count // 8, stride=8), :] for c in range(blocks)], axis=1
        )
        if total is None:
            total = rows
        else:
            total = pltpu.roll(total, blocks * wide - 1, 1) + rows
    return total


def keep_in(acc, first, rows):
    for c in range(acc.shape[0]):
        acc[c, first : first + rows.shape[0], :] = rows[:, c * 128 : (c + 1) * 128]


def back(dims, tile_patch, w_own, meas, keep, *refs):
    q, n_nb, parts, tiles, width, strip, rows, height, ranks, scale = dims
    halos = refs[:n_nb]
    fronts = [refs[n_nb + 3 * i : n_nb + 3 * i + 3] for i in range(parts)]
    band_own, v_own, out, wp, vl, vn, us, acc, acc_z, picks, sem = refs[n_nb + 3 * parts :]
    fetch = pltpu.make_async_copy(tile_patch, picks, sem)
    fetch.start()
    lanes = 2 * strip
    near = ranks * strip
    cells = tiles * ranks
    here = lax.axis_index("field")
    for n in range(n_nb):
        fill(wp, n * strip, halos[n][0, 0])
    fill(wp, n_nb * strip, w_own[0, 0])
    held = {}

    def columns(t):
        for n in range(n_nb):
            first = 0
            for i, (_, cols, _) in enumerate(fronts):
                v = mm(cols[q, t], wp[:, n * strip : (n + 1) * strip])
                vl[n, t, first : first + v.shape[0]] = v.astype(BF)
                first += v.shape[0]
                for r in range(ranks if i == 0 else 0):
                    high, low = split(v[r * height : (r + 1) * height])
                    vn[n, t, r, 0:height, :] = high
                    vn[n, t, r, height : 2 * height, :] = low

    def compare(t):
        total = jnp.zeros((height, width), F32)
        first = 0
        for bands, _, pred in fronts:
            total = total + pred[q, t]
            for r in range(bands.shape[3] // strip):
                for n in range(n_nb):
                    total = total + mm(
                        vl[n, t, first : first + height, :],
                        bands[q, n, t, r * strip : (r + 1) * strip, :],
                    )
                first += height
        cut = slice(t * width, (t + 1) * width)
        residual = keep[:, cut] * (total - meas[0, q, :, cut].astype(F32))
        residual = residual.astype(BF)
        wide = residual.astype(F32)
        pair = jnp.transpose(jnp.concatenate([wide] * (width // height), axis=0)).astype(BF)
        held[t] = residual, pair[:, : 2 * height]

    def spread(t):
        residual = held[t][0]
        for n in range(n_nb + 1):
            bands = band_own[q, t] if n == n_nb else fronts[0][0][q, n, t, :near, :]
            high, low = split(mt(residual, bands))
            for r in range(ranks):
                first = (t * ranks + r) * height
                take = slice(r * strip, (r + 1) * strip)
                span = slice(n * strip, (n + 1) * strip)
                us[first : first + height, span] = high[:, take]
                us[cells * height + first : cells * height + first + height, span] = low[:, take]

    def row_part(t):
        pair = held[t][1]
        x = lax.broadcasted_iota(jnp.int32, (width, strip), 0) + t * width
        j = lax.broadcasted_iota(jnp.int32, (width, strip), 1)
        for r in range(ranks):
            far = jnp.zeros((width, strip), F32)
            for n in range(n_nb):
                mask = below(side_of(n, n_nb, here), j, x)
                far = far + jnp.where(mask, mm(pair, vn[n, t, r]), 0.0)
            both = jnp.concatenate([far, mm(pair, v_own[q, t, r])], axis=1)
            part = pltpu.roll(fold(both), lanes - (t * width + 1), 1)
            keep_in(acc, 8 * (t * ranks + r), part)

    def col_part(t):
        first = t * ranks * height
        some = slice(first, first + ranks * height)
        also = slice(cells * height + first, cells * height + first + ranks * height)
        z = mt(jnp.concatenate([us[some], us[also]], axis=0), wp[...])
        z = z[: ranks * height] + z[ranks * height :]
        for r in range(ranks):
            keep_in(acc_z, 8 * (t * ranks + r), fold(z[r * height : (r + 1) * height]))

    def col_all():
        z = mt(us[...], wp[...])
        z = z[: cells * height] + z[cells * height :]
        for i in range(cells):
            keep_in(acc_z, 8 * i, fold(z[i * height : (i + 1) * height]))

    for t in range(tiles):
        columns(t)
    for t in range(tiles):
        compare(t)
    for t in range(tiles):
        spread(t)
    for t in range(tiles):
        row_part(t)
    col_all()
    fetch.wait()
    row_grads = settle(acc) * scale
    col_grads = settle(acc_z)[:, :lanes] * scale
    for s in range(tiles):
        row = jnp.zeros((ranks, lanes), F32)
        col = jnp.zeros((ranks, lanes), F32)
        for t in range(tiles):
            hit = picks[t] == s
            span = slice(t * ranks, (t + 1) * ranks)
            row = row + jnp.where(hit, row_grads[span], 0.0)
            col = col + jnp.where(hit, col_grads[span], 0.0)
        out[0, s] = row
        out[1, s] = col


def finish(mine, theirs, rows, cols):
    taps = rows.shape[-1]
    for s in range(rows.shape[0]):
        for q in range(rows.shape[1]):
            rows[s, q] = (mine[0, s, q] + theirs[0, s, q])[:, :taps]
            cols[s, q] = (mine[1, s, q] + theirs[1, s, q])[:, :taps]


def body(pattern, measured, row_kernels, col_kernels, tile_patch, sat_tiles):
    _, colours, rows, strip = pattern.shape
    height = measured.shape[2]
    tiles, _, ranks, taps = row_kernels.shape
    width = strip // tiles
    lanes = 2 * strip
    depth = -(-rows // 128) * 128
    fields = lax.axis_size("field")
    banks = lax.axis_size("bank")
    caps = lax.axis_size("cap")
    cells = tiles * ranks

    vmem = pltpu.VMEM
    hbm = pl.BlockSpec(memory_space=pltpu.HBM)
    whole = pl.BlockSpec(memory_space=pltpu.VMEM)
    params = pltpu.CompilerParams(vmem_limit_bytes=24 * 2**20)

    def cost(flops):
        return pl.CostEstimate(flops=flops, bytes_accessed=4 * 10**6, transcendentals=0)

    pattern, measured, row_kernels, col_kernels, tile_patch, sat_tiles = [
        pltpu.with_memory_space_constraint(array, pltpu.HBM)
        for array in (pattern, measured, row_kernels, col_kernels, tile_patch, sat_tiles)
    ]
    *strips, kern, meas, sat = pl.pallas_call(
        prep,
        in_specs=[hbm] * 5,
        out_specs=[whole] * (colours + 3),
        out_shape=[jax.ShapeDtypeStruct((1, 1, rows, strip), BF)] * colours
        + [
            jax.ShapeDtypeStruct((2, tiles, colours, ranks, lanes), BF),
            jax.ShapeDtypeStruct(measured.shape, measured.dtype),
            jax.ShapeDtypeStruct(sat_tiles.shape, sat_tiles.dtype),
        ],
        scratch_shapes=[
            vmem(row_kernels.shape, BF),
            vmem(col_kernels.shape, BF),
            vmem((tiles * colours * ranks, lanes), F32),
            vmem((tiles * colours * ranks, lanes), F32),
            pltpu.SemaphoreType.DMA((colours + 4,)),
        ],
        compiler_params=params,
        cost_estimate=cost(10**7),
        name="prep",
    )(pattern, measured, sat_tiles, row_kernels, col_kernels)

    halos = []
    for part in strips:
        if fields == 2:
            halos.append([exchange(part, "field", 1)])
        else:
            right = [(i, i + 1) for i in range(fields - 1)]
            left = [(i + 1, i) for i in range(fields - 1)]
            halos.append([lax.ppermute(part, "field", right), lax.ppermute(part, "field", left)])
    n_nb = len(halos[0])
    pieces = [kern] + [exchange(kern, "bank", k) for k in range(1, banks)]
    held = len(pieces) * ranks

    own_shapes = [
        ((colours, tiles, ranks * strip, width), BF),
        ((colours, tiles, ranks, 2 * height, strip), BF),
        ((height, strip), F32),
    ]
    cuts = [pieces[:2], pieces[2:]]
    fronts = []
    for i, cut in enumerate(cuts):
        some = len(cut) * ranks
        shapes = [
            ((colours, n_nb, tiles, some * strip, width), BF),
            ((colours, tiles, some * height, depth), BF),
            ((colours, tiles, height, width), F32),
        ]
        if i == 0:
            shapes += own_shapes
        dims = (len(cut), i == 0, colours, n_nb, tiles, width, strip, rows, height, ranks, fields)
        got = pl.pallas_call(
            functools.partial(front, dims),
            in_specs=[hbm] + [whole] * (1 + colours + len(cut)),
            out_specs=[whole] * len(shapes),
            out_shape=[jax.ShapeDtypeStruct(s, d) for s, d in shapes],
            scratch_shapes=[
                vmem((depth, strip), BF),
                vmem((tiles, some * height, strip), BF),
                vmem((n_nb, tiles, strip, width), BF),
                pltpu.SMEM((tiles,), jnp.int32),
                pltpu.SemaphoreType.DMA,
            ],
            compiler_params=params,
            cost_estimate=cost(10**9),
            name=f"front{i}",
        )(tile_patch, sat, *strips, *cut)
        fronts += got[:3]
        if i == 0:
            band_own, v_own, keep = got[3:]

    grads = []
    for q in range(colours):
        dims = (q, n_nb, len(cuts), tiles, width, strip, rows, height, ranks, 1.0 / height)
        grads.append(
            pl.pallas_call(
                functools.partial(back, dims),
                in_specs=[hbm] + [whole] * (5 + n_nb + len(fronts)),
                out_specs=whole,
                out_shape=jax.ShapeDtypeStruct((2, tiles, ranks, lanes), F32),
                scratch_shapes=[
                    vmem((depth, (n_nb + 1) * strip), BF),
                    vmem((n_nb, tiles, held * height, strip), BF),
                    vmem((n_nb, tiles, ranks, 2 * height, strip), BF),
                    vmem((2 * cells * height, (n_nb + 1) * strip), BF),
                    vmem((lanes // 128, 8 * cells, 128), F32),
                    vmem((depth // 128, 8 * cells, 128), F32),
                    pltpu.SMEM((tiles,), jnp.int32),
                    pltpu.SemaphoreType.DMA,
                ],
                compiler_params=params,
                cost_estimate=cost(10**9),
                name=f"back{q}",
            )(tile_patch, strips[q], meas, keep, *halos[q], *fronts, band_own, v_own)
        )
    grads = jnp.stack(grads, axis=2)
    step = caps // 2
    while step > 1:
        grads = grads + exchange(grads, "cap", step)
        step //= 2
    out = jax.ShapeDtypeStruct((tiles, colours, ranks, taps), F32)
    return pl.pallas_call(
        finish,
        in_specs=[whole] * 2,
        out_specs=[whole] * 2,
        out_shape=[out, out],
        compiler_params=params,
        name="finish",
    )(grads, exchange(grads, "cap", 1))


def solution(mesh):
    return jax.shard_map(
        body,
        mesh=mesh,
        in_specs=(
            P("cap", None, None, "field"),
            P("cap", None, None, "field"),
            P("field", None, "bank", None),
            P("field", None, "bank", None),
            P("field"),
            P("cap", None),
        ),
        out_specs=(P("field", None, "bank", None), P("field", None, "bank", None)),
        check_vma=False,
    )
```

```python
import functools

import jax
import jax.numpy as jnp
from jax import lax
from jax.experimental import pallas as pl
from jax.experimental.pallas import tpu as pltpu
from jax.sharding import PartitionSpec as P

TILE = 16
BF = jnp.bfloat16
F32 = jnp.float32


def mm(a, b):
    return jnp.dot(a, b, preferred_element_type=F32)


def mt(a, b):
    return lax.dot_general(a, b, (((1,), (1,)), ((), ())), preferred_element_type=F32)


def split(v):
    high = v.astype(BF)
    return high, (v - high.astype(F32)).astype(BF)


def exchange(cells, axis, step):
    count = lax.axis_size(axis)
    return lax.ppermute(cells, axis, [(i, i ^ step) for i in range(count)])


def fill(dst, at, cells):
    rows, width = cells.shape
    depth = dst.shape[0]
    whole = rows // 16 * 16
    dst[whole:depth, at : at + width] = jnp.zeros((depth - whole, width), BF)
    dst[0:rows, at : at + width] = cells


def below(side, j, x):
    left = (j > x).astype(jnp.int32)
    right = (j < x).astype(jnp.int32)
    return (side * left + (1 - side) * right) > 0


def side_of(n, n_nb, here):
    return here if n_nb == 1 else jnp.int32(1 - n)


def prep(pattern, measured, sat_tiles, row_kernels, col_kernels, *refs):
    colours = pattern.shape[1]
    strips = refs[:colours]
    kern, meas, sat, rows_in, cols_in, rows, cols, sems = refs[colours:]
    tiles, _, ranks, taps = row_kernels.shape
    lanes = rows.shape[1]
    pairs = [(row_kernels, rows_in), (col_kernels, cols_in)]
    pairs += [(pattern.at[:, pl.ds(q, 1)], strips[q]) for q in range(colours)]
    pairs += [(sat_tiles, sat), (measured, meas)]
    copies = [pltpu.make_async_copy(a, b, sems.at[i]) for i, (a, b) in enumerate(pairs)]
    for copy in copies:
        copy.start()
    rows[...] = jnp.zeros(rows.shape, F32)
    cols[...] = jnp.zeros(cols.shape, F32)
    i = lax.broadcasted_iota(jnp.int32, (lanes, lanes), 0)
    m = lax.broadcasted_iota(jnp.int32, (lanes, lanes), 1)
    mirror = (i + m == lanes - 1).astype(F32).astype(BF)
    copies[0].wait()
    copies[1].wait()
    for s in range(tiles):
        for q in range(colours):
            first = (s * colours + q) * ranks
            rows[first : first + ranks, 0:taps] = rows_in[s, q].astype(F32)
            cols[first : first + ranks, 0:taps] = cols_in[s, q].astype(F32)
    mirrored = mm(rows[...].astype(BF), mirror)
    for s in range(tiles):
        for q in range(colours):
            first = (s * colours + q) * ranks
            kern[0, s, q] = mirrored[first : first + ranks].astype(BF)
            kern[1, s, q] = cols[first : first + ranks, :].astype(BF)
    for copy in copies[2:]:
        copy.wait()


def front(dims, tile_patch, sat, *refs):
    count, own, colours, n_nb, tiles, width, strip, rows, height, ranks, fields = dims
    strips = refs[:colours]
    kern = refs[colours : colours + count]
    band_nb, cols, pred = refs[colours + count : colours + count + 3]
    if own:
        turned_own, turned_nb, v_own, keep = refs[colours + count + 3 : -6]
    wp, vl, masks, near, picks, sem = refs[-6:]
    fetch = pltpu.make_async_copy(tile_patch, picks, sem)
    fetch.start()
    lanes = 2 * strip
    depth = wp.shape[0]
    here = lax.axis_index("field")
    for n in range(n_nb):
        side = side_of(n, n_nb, here)
        for t in range(tiles):
            j = lax.broadcasted_iota(jnp.int32, (strip, width), 0)
            x = lax.broadcasted_iota(jnp.int32, (strip, width), 1) + t * width
            masks[n, t] = below(side, j, x).astype(F32).astype(BF)
    if own:
        across = strip // TILE
        boxes = height // TILE * across
        box = lax.broadcasted_iota(jnp.int32, (boxes, 1), 0)
        name = box // across * (across * fields) + here * across + box % across
        hit = jnp.max((sat[...] == name).astype(F32), axis=1, keepdims=True)
        x = lax.broadcasted_iota(jnp.int32, (boxes, strip), 1) // TILE
        wide = jnp.where(x == box % across, hit, 0.0).astype(BF)
        y = lax.broadcasted_iota(jnp.int32, (height, boxes), 0) // TILE
        tall = y == lax.broadcasted_iota(jnp.int32, (height, boxes), 1) // across
        keep[...] = 1.0 - mm(tall.astype(F32).astype(BF), wide)
    fetch.wait()

    for q in range(colours):
        fill(wp, 0, strips[q][0, 0])
        for t in range(tiles):
            pick = picks[t]
            for p in range(count):
                taps = kern[p][1, pick, q].astype(F32)
                taps = jnp.concatenate([taps, jnp.zeros((ranks, depth - lanes), F32)], axis=1)
                for r in range(ranks):
                    first = (p * ranks + r) * height
                    one = jnp.broadcast_to(taps[r : r + 1], (height, depth)).astype(BF)
                    cols[q, t, first : first + height, :] = pltpu.roll(
                        one, 0, 1, stride=1, stride_axis=0
                    )
            v = mm(cols[q, t], wp[...])
            vl[t] = v.astype(BF)
            for r in range(ranks if own else 0):
                high, low = split(v[r * height : (r + 1) * height])
                v_own[q, t, r, 0:height, :] = high
                v_own[q, t, r, height : 2 * height, :] = low
        for t in range(tiles):
            pick = picks[t]
            total = jnp.zeros((height, width), F32)
            for p in range(count):
                taps = kern[p][0, pick, q].astype(F32)
                for r in range(ranks):
                    slot = p * ranks + r
                    at = slot * strip
                    one = jnp.broadcast_to(taps[r : r + 1], (width, lanes)).astype(BF)
                    base = pltpu.roll(one, 0, 1, stride=1, stride_axis=0)
                    blocks = []
                    for a in range(lanes // width):
                        first = (t - a) % (lanes // width) * width
                        blocks.append(base[:, first : first + width])
                    half = len(blocks) // 2
                    for a in range(half):
                        span = slice(a * width, (a + 1) * width)
                        for n in range(n_nb):
                            band_nb[q, n, t, at + a * width : at + (a + 1) * width, :] = (
                                blocks[a] * masks[n, t, span, :]
                            )
                    rest = jnp.concatenate(blocks[half:], axis=0)
                    if own and p == 0:
                        near[t, at : at + strip, :] = rest
                    total = total + mm(vl[t, slot * height : (slot + 1) * height, :], rest)
            pred[q, t] = total
            if own:
                i = lax.broadcasted_iota(jnp.int32, (width, width), 0)
                m = lax.broadcasted_iota(jnp.int32, (width, width), 1)
                same = (i == m).astype(F32).astype(BF)
                turned_own[q, t] = mt(same, near[t]).astype(BF)
                for n in range(n_nb):
                    turned_nb[q, n, t] = mt(same, band_nb[q, n, t, : ranks * strip, :]).astype(BF)


def fold(rows):
    lanes = rows.shape[1]
    total = rows[0:8]
    for g in range(1, rows.shape[0] // 8):
        total = total + pltpu.roll(rows[8 * g : 8 * g + 8], lanes - 8 * g, 1)
    return total


def settle(acc):
    blocks, count, wide = acc.shape
    total = None
    for i in reversed(range(8)):
        rows = jnp.concatenate(
            [acc[c, pl.ds(i, count // 8, stride=8), :] for c in range(blocks)], axis=1
        )
        if total is None:
            total = rows
        else:
            total = pltpu.roll(total, blocks * wide - 1, 1) + rows
    return total


def keep_in(acc, first, rows):
    for c in range(acc.shape[0]):
        acc[c, first : first + rows.shape[0], :] = rows[:, c * 128 : (c + 1) * 128]


def back(dims, tile_patch, w_own, meas, keep, *refs):
    q, n_nb, parts, tiles, width, strip, rows, height, ranks, scale = dims
    halos = refs[:n_nb]
    fronts = [refs[n_nb + 3 * i : n_nb + 3 * i + 3] for i in range(parts)]
    turned_own, turned_nb, v_own = refs[n_nb + 3 * parts : n_nb + 3 * parts + 3]
    out, wp, vl, vn, us, acc, acc_z, picks, sem = refs[n_nb + 3 * parts + 3 :]
    fetch = pltpu.make_async_copy(tile_patch, picks, sem)
    fetch.start()
    lanes = 2 * strip
    cells = tiles * ranks
    here = lax.axis_index("field")
    for n in range(n_nb):
        fill(wp, n * strip, halos[n][0, 0])
    fill(wp, n_nb * strip, w_own[0, 0])
    held = {}

    def columns(t):
        for n in range(n_nb):
            first = 0
            for i, (_, cols, _) in enumerate(fronts):
                v = mm(cols[q, t], wp[:, n * strip : (n + 1) * strip])
                vl[n, t, first : first + v.shape[0]] = v.astype(BF)
                first += v.shape[0]
                for r in range(ranks if i == 0 else 0):
                    high, low = split(v[r * height : (r + 1) * height])
                    vn[n, t, r, 0:height, :] = high
                    vn[n, t, r, height : 2 * height, :] = low

    def compare(t):
        total = jnp.zeros((height, width), F32)
        first = 0
        for bands, _, pred in fronts:
            total = total + pred[q, t]
            for r in range(bands.shape[3] // strip):
                for n in range(n_nb):
                    total = total + mm(
                        vl[n, t, first : first + height, :],
                        bands[q, n, t, r * strip : (r + 1) * strip, :],
                    )
                first += height
        cut = slice(t * width, (t + 1) * width)
        residual = keep[:, cut] * (total - meas[0, q, :, cut].astype(F32))
        residual = residual.astype(BF)
        wide = residual.astype(F32)
        pair = jnp.transpose(jnp.concatenate([wide] * (width // height), axis=0)).astype(BF)
        held[t] = residual, pair[:, : 2 * height]

    def spread(t):
        residual = held[t][0]
        for n in range(n_nb + 1):
            bands = turned_own[q, t] if n == n_nb else turned_nb[q, n, t]
            high, low = split(mm(residual, bands))
            for r in range(ranks):
                first = (t * ranks + r) * height
                take = slice(r * strip, (r + 1) * strip)
                span = slice(n * strip, (n + 1) * strip)
                us[first : first + height, span] = high[:, take]
                us[cells * height + first : cells * height + first + height, span] = low[:, take]

    def row_part(t):
        pair = held[t][1]
        x = lax.broadcasted_iota(jnp.int32, (width, strip), 0) + t * width
        j = lax.broadcasted_iota(jnp.int32, (width, strip), 1)
        for r in range(ranks):
            far = jnp.zeros((width, strip), F32)
            for n in range(n_nb):
                mask = below(side_of(n, n_nb, here), j, x)
                far = far + jnp.where(mask, mm(pair, vn[n, t, r]), 0.0)
            both = jnp.concatenate([far, mm(pair, v_own[q, t, r])], axis=1)
            part = pltpu.roll(fold(both), lanes - (t * width + 1), 1)
            keep_in(acc, 8 * (t * ranks + r), part)

    def col_part(t):
        first = t * ranks * height
        some = slice(first, first + ranks * height)
        also = slice(cells * height + first, cells * height + first + ranks * height)
        z = mt(jnp.concatenate([us[some], us[also]], axis=0), wp[...])
        z = z[: ranks * height] + z[ranks * height :]
        for r in range(ranks):
            keep_in(acc_z, 8 * (t * ranks + r), fold(z[r * height : (r + 1) * height]))

    def col_all():
        z = mt(us[...], wp[...])
        z = z[: cells * height] + z[cells * height :]
        for i in range(cells):
            keep_in(acc_z, 8 * i, fold(z[i * height : (i + 1) * height]))

    for t in range(tiles):
        columns(t)
    for t in range(tiles):
        compare(t)
    for t in range(tiles):
        spread(t)
    for t in range(tiles):
        row_part(t)
    col_all()
    fetch.wait()
    row_grads = settle(acc) * scale
    col_grads = settle(acc_z)[:, :lanes] * scale
    for s in range(tiles):
        row = jnp.zeros((ranks, lanes), F32)
        col = jnp.zeros((ranks, lanes), F32)
        for t in range(tiles):
            hit = picks[t] == s
            span = slice(t * ranks, (t + 1) * ranks)
            row = row + jnp.where(hit, row_grads[span], 0.0)
            col = col + jnp.where(hit, col_grads[span], 0.0)
        out[0, s] = row
        out[1, s] = col


def finish(mine, theirs, rows, cols):
    taps = rows.shape[-1]
    for s in range(rows.shape[0]):
        for q in range(rows.shape[1]):
            rows[s, q] = (mine[0, s, q] + theirs[0, s, q])[:, :taps]
            cols[s, q] = (mine[1, s, q] + theirs[1, s, q])[:, :taps]


def body(pattern, measured, row_kernels, col_kernels, tile_patch, sat_tiles):
    _, colours, rows, strip = pattern.shape
    height = measured.shape[2]
    tiles, _, ranks, taps = row_kernels.shape
    width = strip // tiles
    lanes = 2 * strip
    depth = -(-rows // 128) * 128
    fields = lax.axis_size("field")
    banks = lax.axis_size("bank")
    caps = lax.axis_size("cap")
    cells = tiles * ranks

    vmem = pltpu.VMEM
    hbm = pl.BlockSpec(memory_space=pltpu.HBM)
    whole = pl.BlockSpec(memory_space=pltpu.VMEM)
    params = pltpu.CompilerParams(vmem_limit_bytes=24 * 2**20)

    def cost(flops):
        return pl.CostEstimate(flops=flops, bytes_accessed=4 * 10**6, transcendentals=0)

    pattern, measured, row_kernels, col_kernels, tile_patch, sat_tiles = [
        pltpu.with_memory_space_constraint(array, pltpu.HBM)
        for array in (pattern, measured, row_kernels, col_kernels, tile_patch, sat_tiles)
    ]
    *strips, kern, meas, sat = pl.pallas_call(
        prep,
        in_specs=[hbm] * 5,
        out_specs=[whole] * (colours + 3),
        out_shape=[jax.ShapeDtypeStruct((1, 1, rows, strip), BF)] * colours
        + [
            jax.ShapeDtypeStruct((2, tiles, colours, ranks, lanes), BF),
            jax.ShapeDtypeStruct(measured.shape, measured.dtype),
            jax.ShapeDtypeStruct(sat_tiles.shape, sat_tiles.dtype),
        ],
        scratch_shapes=[
            vmem(row_kernels.shape, BF),
            vmem(col_kernels.shape, BF),
            vmem((tiles * colours * ranks, lanes), F32),
            vmem((tiles * colours * ranks, lanes), F32),
            pltpu.SemaphoreType.DMA((colours + 4,)),
        ],
        compiler_params=params,
        cost_estimate=cost(10**7),
        name="prep",
    )(pattern, measured, sat_tiles, row_kernels, col_kernels)

    halos = []
    for part in strips:
        if fields == 2:
            halos.append([exchange(part, "field", 1)])
        else:
            right = [(i, i + 1) for i in range(fields - 1)]
            left = [(i + 1, i) for i in range(fields - 1)]
            halos.append([lax.ppermute(part, "field", right), lax.ppermute(part, "field", left)])
    n_nb = len(halos[0])
    pieces = [kern] + [exchange(kern, "bank", k) for k in range(1, banks)]
    held = len(pieces) * ranks

    own_shapes = [
        ((colours, tiles, width, ranks * strip), BF),
        ((colours, n_nb, tiles, width, ranks * strip), BF),
        ((colours, tiles, ranks, 2 * height, strip), BF),
        ((height, strip), F32),
    ]
    cuts = [pieces[:2], pieces[2:]]
    fronts = []
    for i, cut in enumerate(cuts):
        some = len(cut) * ranks
        shapes = [
            ((colours, n_nb, tiles, some * strip, width), BF),
            ((colours, tiles, some * height, depth), BF),
            ((colours, tiles, height, width), F32),
        ]
        if i == 0:
            shapes += own_shapes
        dims = (len(cut), i == 0, colours, n_nb, tiles, width, strip, rows, height, ranks, fields)
        got = pl.pallas_call(
            functools.partial(front, dims),
            in_specs=[hbm] + [whole] * (1 + colours + len(cut)),
            out_specs=[whole] * len(shapes),
            out_shape=[jax.ShapeDtypeStruct(s, d) for s, d in shapes],
            scratch_shapes=[
                vmem((depth, strip), BF),
                vmem((tiles, some * height, strip), BF),
                vmem((n_nb, tiles, strip, width), BF),
                vmem((tiles, ranks * strip, width), BF),
                pltpu.SMEM((tiles,), jnp.int32),
                pltpu.SemaphoreType.DMA,
            ],
            compiler_params=params,
            cost_estimate=cost(10**9),
            name=f"front{i}",
        )(tile_patch, sat, *strips, *cut)
        fronts += got[:3]
        if i == 0:
            *extras, keep = got[3:]

    grads = []
    for q in range(colours):
        dims = (q, n_nb, len(cuts), tiles, width, strip, rows, height, ranks, 1.0 / height)
        grads.append(
            pl.pallas_call(
                functools.partial(back, dims),
                in_specs=[hbm] + [whole] * (6 + n_nb + len(fronts)),
                out_specs=whole,
                out_shape=jax.ShapeDtypeStruct((2, tiles, ranks, lanes), F32),
                scratch_shapes=[
                    vmem((depth, (n_nb + 1) * strip), BF),
                    vmem((n_nb, tiles, held * height, strip), BF),
                    vmem((n_nb, tiles, ranks, 2 * height, strip), BF),
                    vmem((2 * cells * height, (n_nb + 1) * strip), BF),
                    vmem((lanes // 128, 8 * cells, 128), F32),
                    vmem((depth // 128, 8 * cells, 128), F32),
                    pltpu.SMEM((tiles,), jnp.int32),
                    pltpu.SemaphoreType.DMA,
                ],
                compiler_params=params,
                cost_estimate=cost(10**9),
                name=f"back{q}",
            )(tile_patch, strips[q], meas, keep, *halos[q], *fronts, *extras)
        )
    grads = jnp.stack(grads, axis=2)
    step = caps // 2
    while step > 1:
        grads = grads + exchange(grads, "cap", step)
        step //= 2
    out = jax.ShapeDtypeStruct((tiles, colours, ranks, taps), F32)
    return pl.pallas_call(
        finish,
        in_specs=[whole] * 2,
        out_specs=[whole] * 2,
        out_shape=[out, out],
        compiler_params=params,
        name="finish",
    )(grads, exchange(grads, "cap", 1))


def solution(mesh):
    return jax.shard_map(
        body,
        mesh=mesh,
        in_specs=(
            P("cap", None, None, "field"),
            P("cap", None, None, "field"),
            P("field", None, "bank", None),
            P("field", None, "bank", None),
            P("field"),
            P("cap", None),
        ),
        out_specs=(P("field", None, "bank", None), P("field", None, "bank", None)),
        check_vma=False,
    )
```
